32 devices in a mesh: band: 4 (over y, core), pgroup: 8 (over z, x).
Axes of the slice: x: 2, y: 2, z: 4, core: 2. Of those that a mesh axis runs over, the one named last changes fastest.
Arguments:
- state: float32 [128, 256, 512], P('pgroup', 'band'), may hold values from -6 to 6
- forcing: float32 [256, 512], P('band'), may hold values from -3 to 3
- parents: int32 [64, 128], P('band'), may hold values from 0 to 127, as said below
- taper_index: int32 [256], P('band'), may hold values from 0 to 7
Outputs:
- analysis: float32 [128, 256, 512], P('pgroup', 'band')
The draws below stay inside these ranges and needn't reach their ends.
Inputs may be any that keep to these rules, and one draw needn't show every extreme that they name: In every patch, the parents of the 16 particles k with k // 16 = g are distinct and come from exactly 8 groups (a group holds the particles j with the same j // 16), exactly 2 from each of them, for every patch and every g.
All inputs are finite; a program needn't handle non-finite values.
Results may differ from the reference program's by a relative error of at most 0.000071.
Values sent between devices are 32-bit elements; how exact they have to be, the bound alone decides.
A program may use at most 64 MiB of HBM per device.

```python
import jax
import jax.numpy as jnp
from jax import lax

NX = 512
PART_DEV = 16
PATCH_ROWS = 4
STEPS = 6
CAP = 2
NY = 256
PARTICLES = 128
PATCHES = 64


def draw_parents(key, part):
    groups = PARTICLES // PART_DEV
    sources = PART_DEV // CAP
    pairs = PATCHES * groups
    key_src, key_loc, key_mix = jax.random.split(key, 3)
    chosen_src = jax.vmap(lambda k: jax.random.permutation(k, groups))(jax.random.split(key_src, pairs))[:, :sources]
    chosen_loc = jax.vmap(lambda k: jax.random.permutation(k, PART_DEV))(jax.random.split(key_loc, pairs * sources)).reshape(pairs, sources, PART_DEV)
    slot = jnp.arange(PART_DEV, dtype=jnp.int32)
    position = slot // CAP
    order = slot % CAP
    owner = chosen_src[:, position]
    within = chosen_loc[:, position, order]
    parent = owner * PART_DEV + within
    shuffle = jax.vmap(lambda k: jax.random.permutation(k, PART_DEV))(jax.random.split(key_mix, pairs))
    parent = jnp.take_along_axis(parent, shuffle, axis=1)
    return parent.reshape(PATCHES, groups * PART_DEV).astype(jnp.int32)


def touch_ends(entries, rng, least, top_value):
    longest = entries.shape.index(max(entries.shape))
    spots = []
    for shift in (0, 1):
        where = [jax.random.randint(jax.random.fold_in(rng, axis), (), 0, length) for axis, length in enumerate(entries.shape)]
        where[longest] = (where[longest] + shift) % entries.shape[longest]
        spots.append(tuple(where))
    return entries.at[spots[0]].set(least).at[spots[1]].set(top_value)


def block_scale(rng, extent, pieces, least, high):
    level, own = 1.0, jax.random.fold_in(rng, 6)
    for dim, blocks in pieces:
        heights = jnp.exp(jax.random.uniform(jax.random.fold_in(own, dim), (blocks,), jnp.float32, least / len(pieces), high / len(pieces)))
        level = level * jnp.repeat(heights, extent[dim] // blocks).reshape([-1 if axis == dim else 1 for axis in range(len(extent))])
    return level


def normal_values(own_key, shape, deviation, reach, cuts=(), kind=jnp.bfloat16):
    drawn = deviation * jax.random.normal(own_key, shape, jnp.float32)
    if cuts:
        drawn = drawn * block_scale(own_key, shape, cuts, -0.22, 0.18)
    return jnp.clip(drawn, -reach, reach).astype(kind)


def setup_inputs(seed: int = 0) -> dict:
    arg_keys = jax.random.split(jax.random.key(seed), 5)
    state = normal_values(arg_keys[0], (PARTICLES, NY, NX), 1.0, 6.0, ((0, 8), (1, 4)), jnp.float32)
    forcing = normal_values(arg_keys[1], (NY, NX), 0.3, 3.0, ((0, 4),), jnp.float32)
    parents = draw_parents(jax.random.fold_in(arg_keys[4], 71), 0)
    taper_index = touch_ends(jax.random.randint(arg_keys[3], (NY,), 0, 8), jax.random.fold_in(arg_keys[3], 1), 0, 7).astype(jnp.int32)
    return {"state": state, "forcing": forcing, "parents": parents, "taper_index": taper_index}


advect_x = 0.05
advect_y = 0.1
diffuse = 0.15
taper_kinds = 8


def advect(padded, drive):
    center = padded[:, 1:-1]
    north = padded[:, 2:]
    south = padded[:, :-2]
    east = jnp.roll(center, -1, axis=2)
    west = jnp.roll(center, 1, axis=2)
    return center - advect_x * center * (east - west) - advect_y * (north - south) + diffuse * (east + west + north + south - 4.0 * center) + drive[None]


def taper_weights(taper_rows):
    offsets = jnp.arange(5, dtype=jnp.float32) - 2.0
    rates = 0.2 * (jnp.arange(taper_kinds, dtype=jnp.float32) + 1.0)
    raw_table = jnp.exp(-rates[:, None] * offsets[None, :] * offsets[None, :])
    table = raw_table / jnp.sum(raw_table, axis=1, keepdims=True)
    onehot = (taper_rows[:, None] == jnp.arange(taper_kinds, dtype=jnp.int32)[None, :]).astype(jnp.float32)
    return jnp.dot(onehot, table, precision=lax.Precision.HIGHEST)


def blend(padded, weights):
    rows = weights.shape[0]
    total = weights[:, 0][None, :, None] * padded[:, 0:rows]
    for offset in range(1, 5):
        total = total + weights[:, offset][None, :, None] * padded[:, offset:offset + rows]
    return total


def reference(state, forcing, parents, taper_index):
    field = state
    for repeat in range(STEPS):
        field = advect(jnp.pad(field, ((0, 0), (1, 1), (0, 0))), forcing)
    blocks = field.reshape(PARTICLES, PATCHES, PATCH_ROWS * NX)
    picked = blocks[parents.T, jnp.arange(PATCHES, dtype=jnp.int32)[None, :]]
    field = picked.reshape(PARTICLES, NY, NX)
    field = blend(jnp.pad(field, ((0, 0), (2, 2), (0, 0))), taper_weights(taper_index))
    for repeat in range(STEPS):
        field = advect(jnp.pad(field, ((0, 0), (1, 1), (0, 0))), forcing)
    return field
```

```python
import functools

import jax
import jax.numpy as jnp
from jax import lax
from jax.experimental import pallas as pl
from jax.experimental.pallas import tpu as pltpu
from jax.sharding import PartitionSpec as P

PATCH_ROWS = 4
STEPS = 6
CAP = 2
LANES = 128
TILE = 8
SCALE = 0.05
MESH = pl.DeviceIdType.MESH
f32 = jnp.float32


def cut(low, high, most=TILE):
    pieces = -(-(high - low) // most)
    marks = [low + (high - low) * i // pieces for i in range(pieces + 1)]
    return [(a, b - a) for a, b in zip(marks[:-1], marks[1:])]


def split(value):
    return [value[..., b * LANES : (b + 1) * LANES] for b in range(value.shape[-1] // LANES)]


def kernel(
    bands, groups, chunks, state, forcing, parents, taper, out,
    st, fo, par, kinds, table, lookup, first, field, mixed, drive, weight,
    s_lo, s_hi, f_lo, f_hi, t_lo, t_hi, send,
    in_sem, halo_send, halo_recv, send_sem, recv_sem, *recvs,
):
    band, me = lax.axis_index("band"), lax.axis_index("pgroup")
    per_dev, tiles, blocks = state.shape[:3]
    extent, packs = tiles * TILE, per_dev // TILE
    patches = par.shape[0]
    quarter = tiles // 4
    has_low, has_high = band > 0, band < bands - 1
    up, down = lax.rem(band + 1, bands), lax.rem(band + bands - 1, bands)

    barrier = pltpu.get_barrier_semaphore()
    for step in range(1, groups):
        pl.semaphore_signal(
            barrier, inc=1, device_id={"pgroup": lax.rem(me + step, groups)}, device_id_type=MESH
        )

    @pl.when(has_low)
    def _():
        pl.semaphore_signal(barrier, inc=1, device_id={"band": down}, device_id_type=MESH)

    @pl.when(has_high)
    def _():
        pl.semaphore_signal(barrier, inc=1, device_id={"band": up}, device_id_type=MESH)

    def fetch(index, low, high):
        return pltpu.make_async_copy(
            state.at[:, low:high], st.at[:, low:high], in_sem.at[index]
        )

    inputs = [
        fetch(0, 2 * quarter - 2, 2 * quarter + 1),
        fetch(1, 0, 2 * quarter - 2),
        fetch(2, 2 * quarter + 1, tiles),
        pltpu.make_async_copy(forcing, fo, in_sem.at[3]),
        pltpu.make_async_copy(parents, par, in_sem.at[4]),
    ]
    for index in (4, 0, 3, 1, 2):
        inputs[index].start()

    def halo(index, src, low, high, last, start):
        upward = pltpu.make_async_remote_copy(
            src_ref=src.at[last], dst_ref=low,
            send_sem=halo_send.at[2 * index], recv_sem=halo_recv.at[2 * index],
            device_id={"band": up}, device_id_type=MESH,
        )
        downward = pltpu.make_async_remote_copy(
            src_ref=src.at[start], dst_ref=high,
            send_sem=halo_send.at[2 * index + 1], recv_sem=halo_recv.at[2 * index + 1],
            device_id={"band": down}, device_id_type=MESH,
        )
        return upward, downward

    every = slice(None)
    bottom, top = slice(0, TILE), slice(extent - TILE, extent)
    edges = [
        halo(0, state, s_lo, s_hi, (every, slice(tiles - 1, tiles)), (every, slice(0, 1))),
        halo(1, forcing, f_lo, f_hi, (top,), (bottom,)),
        halo(2, kinds, t_lo, t_hi, (top,), (bottom,)),
    ]
    middle = halo(
        3, mixed, mixed.at[:, 0:TILE], mixed.at[:, extent + TILE : extent + 2 * TILE],
        (every, slice(extent, extent + TILE)), (every, slice(TILE, 2 * TILE)),
    )

    @pl.when(jnp.logical_not(has_low))
    def _():
        for ref in (s_lo, f_lo, t_lo):
            ref[...] = jnp.zeros_like(ref)
        mixed[:, 0:TILE] = jnp.zeros((packs, TILE, TILE, blocks * LANES), f32)

    @pl.when(jnp.logical_not(has_high))
    def _():
        for ref in (s_hi, f_hi, t_hi):
            ref[...] = jnp.zeros_like(ref)
        mixed[:, extent + TILE : extent + 2 * TILE] = jnp.zeros(
            (packs, TILE, TILE, blocks * LANES), f32
        )

    lane = lax.broadcasted_iota(jnp.int32, (TILE * TILE, LANES), 1)
    run = LANES // blocks
    deal = (lane % run) * blocks + lane // run
    undeal = (lane % blocks) * run + lane // blocks

    def exchange(parts):
        parts = list(parts)
        span, count = LANES // 2, blocks // 2
        while count:
            near = (lane[: parts[0].shape[0]] & span) == 0
            for j in range(blocks):
                if j & count:
                    continue
                a, b = parts[j], parts[j + count]
                parts[j] = jnp.where(near, a, pltpu.roll(b, span, 1))
                parts[j + count] = jnp.where(near, pltpu.roll(a, LANES - span, 1), b)
            span, count = span // 2, count // 2
        return parts

    def interleave(parts):
        return exchange([jnp.take_along_axis(part, deal[: part.shape[0]], axis=1) for part in parts])

    def restore(parts):
        return [jnp.take_along_axis(part, undeal, axis=1) for part in exchange(parts)]

    def tables():
        value = par[...]
        spot = lax.broadcasted_iota(jnp.int32, value.shape, 1) % per_dev
        owner, within = value // per_dev, value % per_dev
        mine = owner == me
        least = jnp.where(mine, within, per_dev - 1)
        most = jnp.where(mine, within, 0)
        reach = 1
        while reach < per_dev:
            least = jnp.minimum(least, pltpu.roll(least, value.shape[1] - reach, 1))
            most = jnp.maximum(most, pltpu.roll(most, value.shape[1] - reach, 1))
            reach *= 2
        rank = jnp.zeros_like(value)
        for reach in range(1, per_dev):
            ahead = pltpu.roll(value, value.shape[1] - reach, 1)
            behind = pltpu.roll(value, per_dev - reach, 1)
            other = jnp.where(spot + reach < per_dev, ahead, behind)
            below = (other // per_dev == owner) & (other < value)
            rank = jnp.where(below, 1, rank)
        table[0] = least
        table[1] = most
        table[2] = owner
        table[3] = rank

    def piece(low, mid, high, row):
        if row < 0:
            return low, row + TILE
        if row >= extent:
            return high, row - extent
        return mid, row

    sub = lax.broadcasted_iota(jnp.int32, (TILE, LANES), 0)

    def fill_kinds():
        for tile in range(tiles):
            value = jnp.zeros((TILE, LANES), f32)
            for r in range(TILE):
                value = jnp.where(sub == r, taper[tile * TILE + r].astype(f32), value)
            kinds[tile * TILE : (tile + 1) * TILE] = value

    def fill_drive(low, high):
        for tile in range(low, high):
            ref, at = piece(f_lo, fo, f_hi, tile * TILE)
            parts = interleave([SCALE * part for part in split(ref[at : at + TILE])])
            for b, part in enumerate(parts):
                for r in range(TILE):
                    drive[(tile + 1) * TILE + r, :, b * LANES : (b + 1) * LANES] = (
                        jnp.broadcast_to(part[r : r + 1], (TILE, LANES))
                    )

    def fill_weight(low, high):
        for row in range(low, high):
            ref, at = piece(t_lo, kinds, t_hi, row)
            kind = jnp.broadcast_to(ref[pl.ds(at, 1), :], (TILE, LANES)) + 1.0
            near, far = jnp.exp(-0.2 * kind), jnp.exp(-0.8 * kind)
            scale = 1.0 / (1.0 + 2.0 * near + 2.0 * far)
            weight[0, row + TILE] = scale
            weight[1, row + TILE] = near * scale
            weight[2, row + TILE] = far * scale

    def clear(ref, low, high):
        if low < 0:
            ref[:, TILE - 1] = jnp.where(has_low, ref[:, TILE - 1], 0.0)
        if high > extent:
            ref[:, TILE + extent] = jnp.where(has_high, ref[:, TILE + extent], 0.0)

    def bounds(job, step):
        low, high, left, right = job
        rest = STEPS - step
        return low + (rest if left else -rest), high - (rest if right else -rest)

    def advance(source, target, pack, at, size):
        c = split(source[pack, at : at + size])
        n = split(source[pack, at + 1 : at + size + 1])
        s = split(source[pack, at - 1 : at + size - 1])
        d = split(drive[at : at + size])
        wrap_e = pltpu.roll(c[0], LANES - 1, 2)
        wrap_w = pltpu.roll(c[-1], 1, 2)
        for b in range(blocks):
            e = c[b + 1] if b < blocks - 1 else wrap_e
            w = c[b - 1] if b else wrap_w
            target[pack, at : at + size, :, b * LANES : (b + 1) * LANES] = (
                c[b] * (0.4 - (e - w)) + 0.15 * (e + w)
            ) + ((0.05 * n[b] + 0.25 * s[b]) + d[b])

    def sweep(job):
        for step in range(1, STEPS + 1):
            low, high = bounds(job, step)
            source, target = field.at[(step - 1) % 2], field.at[step % 2]
            for row, size in cut(low, high):
                for pack in range(packs):
                    advance(source, target, pack, row + TILE, size)
            if step < STEPS:
                clear(target, low, high)

    def load(low, high):
        for tile in range(low, high):
            if tile < 0:
                ref, at = s_lo, 0
            elif tile >= tiles:
                ref, at = s_hi, 0
            else:
                ref, at = st, tile
            for pack in range(packs):
                parts = interleave(
                    [
                        jnp.swapaxes(
                            SCALE * ref[pack * TILE : (pack + 1) * TILE, at, b], 0, 1
                        ).reshape(TILE * TILE, LANES)
                        for b in range(blocks)
                    ]
                )
                for b, part in enumerate(parts):
                    field[
                        0, pack, (tile + 1) * TILE : (tile + 2) * TILE, :,
                        b * LANES : (b + 1) * LANES,
                    ] = part.reshape(TILE, TILE, LANES)

    upper = lax.broadcasted_iota(jnp.int32, (blocks, TILE, LANES), 1) < PATCH_ROWS

    def gather(index):
        base, count = chunks[index]
        for tile in range(base, base + count):
            for pack in range(packs):
                for b, part in enumerate(
                    split(field[0, pack, (tile + 1) * TILE : (tile + 2) * TILE])
                ):
                    first[pack * TILE : (pack + 1) * TILE, tile, b] = jnp.swapaxes(part, 0, 1)
        for tile in range(base, base + count):

            def body(g, carry, tile=tile):
                for slot in range(CAP):
                    even = lookup[slot, 2 * tile, g * per_dev]
                    odd = lookup[slot, 2 * tile + 1, g * per_dev]
                    send[g, tile, slot] = jnp.where(upper, first[even, tile], first[odd, tile])
                return carry

            lax.fori_loop(0, groups, body, 0)

    def scatter(index):
        base, count = chunks[index]
        recv = recvs[index]
        for tile in range(base, base + count):
            j = tile - base
            for pack in range(packs):
                children = []
                for k in range(pack * TILE, (pack + 1) * TILE):
                    at = me * per_dev + k
                    even = recv[lookup[2, 2 * tile, at], j, lookup[3, 2 * tile, at]]
                    odd = recv[lookup[2, 2 * tile + 1, at], j, lookup[3, 2 * tile + 1, at]]
                    children.append(jnp.where(upper, even, odd))
                for b in range(blocks):
                    mixed[
                        pack, (tile + 1) * TILE : (tile + 2) * TILE, :,
                        b * LANES : (b + 1) * LANES,
                    ] = jnp.swapaxes(jnp.stack([child[b] for child in children]), 0, 1)

    def blend(job):
        low, high = bounds(job, 0)
        for row, size in cut(low, high):
            at = row + TILE
            w = [weight[j, at : at + size] for j in range(3)]
            for pack in range(packs):
                near = [split(mixed[pack, at + j : at + j + size]) for j in range(-2, 3)]
                for b in range(blocks):
                    field[0, pack, at : at + size, :, b * LANES : (b + 1) * LANES] = (
                        w[0] * near[2][b]
                        + w[1] * (near[1][b] + near[3][b])
                        + w[2] * (near[0][b] + near[4][b])
                    )
        clear(field.at[0], low, high)

    def finish(low, high):
        for tile in range(low, high):
            for pack in range(packs):
                parts = restore(
                    [
                        part.reshape(TILE * TILE, LANES)
                        for part in split(field[0, pack, (tile + 1) * TILE : (tile + 2) * TILE])
                    ]
                )
                for b, part in enumerate(parts):
                    out[pack * TILE : (pack + 1) * TILE, tile, b] = jnp.swapaxes(
                        part.reshape(TILE, TILE, LANES), 0, 1
                    )

    shifts = sorted(range(1, groups), key=lambda i: -min(i, groups - i))

    def exchange_out(index):
        base, count = chunks[index]
        part = slice(base, base + count)
        for shift in shifts:
            to = lax.rem(me + shift, groups)
            pltpu.make_async_remote_copy(
                src_ref=send.at[to, part], dst_ref=recvs[index].at[me],
                send_sem=send_sem.at[0], recv_sem=recv_sem.at[index],
                device_id={"pgroup": to}, device_id_type=MESH,
            ).start()
        pltpu.make_async_copy(
            send.at[me, part], recvs[index].at[me], recv_sem.at[index]
        ).start()

    def exchange_in(index):
        base, count = chunks[index]
        part = slice(base, base + count)
        pltpu.make_async_copy(send.at[:, part], recvs[index], recv_sem.at[index]).wait()

    q = quarter
    fill_kinds()
    inputs[4].wait()
    tables()
    to_lookup = pltpu.make_async_copy(table, lookup, in_sem.at[5])
    to_lookup.start()
    inputs[3].wait()
    fill_drive(q, 3 * q)
    inputs[0].wait()
    load(2 * q - 2, 2 * q + 1)
    sweep((TILE * (2 * q - 1), TILE * 2 * q, False, False))
    to_lookup.wait()
    gather(0)
    pl.semaphore_wait(
        barrier, groups - 1 + has_low.astype(jnp.int32) + has_high.astype(jnp.int32)
    )

    @pl.when(has_high)
    def _():
        for upward, _ in edges:
            upward.start()

    @pl.when(has_low)
    def _():
        for _, downward in edges:
            downward.start()

    exchange_out(0)
    inputs[1].wait()
    fill_drive(0, q)
    load(q - 1, 2 * q - 2)
    sweep((TILE * q, TILE * (2 * q - 1), False, True))
    gather(1)
    exchange_out(1)
    inputs[2].wait()
    fill_drive(3 * q, tiles)

    @pl.when(has_low)
    def _():
        for upward, _ in edges:
            upward.wait_recv()

    @pl.when(has_high)
    def _():
        for _, downward in edges:
            downward.wait_recv()

    fill_drive(-1, 0)
    fill_drive(tiles, tiles + 1)
    load(-1, q - 1)
    sweep((0, TILE * q, False, True))
    gather(2)
    exchange_out(2)
    load(3 * q - 1, tiles + 1)
    sweep((TILE * 3 * q, extent, False, False))
    gather(3)
    exchange_out(3)
    load(2 * q + 1, 3 * q - 1)
    sweep((TILE * 2 * q, TILE * 3 * q, True, True))
    gather(4)
    exchange_out(4)
    gather(5)
    exchange_out(5)
    fill_weight(-TILE, extent + TILE)

    def second(job):
        blend(job)
        sweep(job)
        finish(job[0] // TILE, job[1] // TILE)

    for index in range(3):
        exchange_in(index)
        scatter(index)

    @pl.when(has_low)
    def _():
        middle[1].start()

    second((TILE, TILE * (2 * q - 1), False, False))
    exchange_in(3)
    scatter(3)

    @pl.when(has_high)
    def _():
        middle[0].start()

    @pl.when(has_high)
    def _():
        middle[1].wait_recv()

    second((TILE * (3 * q + 1), extent, False, False))
    exchange_in(4)
    scatter(4)
    second((TILE * (2 * q - 1), TILE * (3 * q - 2), True, False))

    @pl.when(has_low)
    def _():
        middle[0].wait_recv()

    second((0, TILE, False, True))
    exchange_in(5)
    scatter(5)
    second((TILE * (3 * q - 2), TILE * (3 * q + 1), True, True))

    @pl.when(has_high)
    def _():
        for upward, _ in edges:
            upward.wait_send()
        middle[0].wait_send()

    @pl.when(has_low)
    def _():
        for _, downward in edges:
            downward.wait_send()
        middle[1].wait_send()

    sent = slice(0, groups - 1)
    pltpu.make_async_remote_copy(
        src_ref=send.at[sent], dst_ref=send.at[sent],
        send_sem=send_sem.at[0], recv_sem=recv_sem.at[0],
        device_id={"pgroup": lax.rem(me + 1, groups)}, device_id_type=MESH,
    ).wait_send()


def on_device(state, forcing, parents, taper_index):
    per_dev, extent, width = state.shape
    bands, groups = lax.axis_size("band"), lax.axis_size("pgroup")
    blocks, tiles, packs = width // LANES, extent // TILE, per_dev // TILE
    state = state.reshape(per_dev, tiles, TILE, blocks, LANES).transpose(0, 1, 3, 2, 4)
    q = tiles // 4
    chunks = [
        (2 * q - 1, 1),
        (q, q - 1),
        (0, q),
        (3 * q, q),
        (2 * q, q - 1),
        (3 * q - 1, 1),
    ]
    rows = extent + 2 * TILE
    edge = (per_dev, 1, blocks, TILE, LANES)
    slot = (CAP, blocks, TILE, LANES)
    vmem, smem = pl.BlockSpec(memory_space=pltpu.VMEM), pl.BlockSpec(memory_space=pltpu.SMEM)
    hbm = pl.BlockSpec(memory_space=pltpu.HBM)
    out = pl.pallas_call(
        functools.partial(kernel, bands, groups, chunks),
        out_shape=jax.ShapeDtypeStruct(state.shape, f32),
        in_specs=[hbm, hbm, hbm, smem],
        out_specs=vmem,
        scratch_shapes=[
            pltpu.VMEM(state.shape, f32),
            pltpu.VMEM(forcing.shape, f32),
            pltpu.VMEM(parents.shape, jnp.int32),
            pltpu.VMEM((extent, LANES), f32),
            pltpu.VMEM((4, *parents.shape), jnp.int32),
            pltpu.SMEM((4, *parents.shape), jnp.int32),
            pltpu.VMEM(state.shape, f32),
            pltpu.VMEM((2, packs, rows, TILE, width), f32),
            pltpu.VMEM((packs, rows, TILE, width), f32),
            pltpu.VMEM((rows, TILE, width), f32),
            pltpu.VMEM((3, rows, TILE, LANES), f32),
            pltpu.VMEM(edge, f32),
            pltpu.VMEM(edge, f32),
            pltpu.VMEM((TILE, width), f32),
            pltpu.VMEM((TILE, width), f32),
            pltpu.VMEM((TILE, LANES), f32),
            pltpu.VMEM((TILE, LANES), f32),
            pltpu.VMEM((groups, tiles, *slot), f32),
            pltpu.SemaphoreType.DMA((6,)),
            pltpu.SemaphoreType.DMA((8,)),
            pltpu.SemaphoreType.DMA((8,)),
            pltpu.SemaphoreType.DMA((1,)),
            pltpu.SemaphoreType.DMA((len(chunks),)),
            *[pltpu.VMEM((groups, count, *slot), f32) for _, count in chunks],
        ],
        compiler_params=pltpu.CompilerParams(
            collective_id=0, has_side_effects=True, vmem_limit_bytes=34 << 20
        ),
        name="filter_step",
    )(state, forcing, parents, taper_index)
    out = out * (1.0 / SCALE)
    return out.transpose(0, 1, 3, 2, 4).reshape(per_dev, extent, width)


def solution(mesh):
    return jax.shard_map(
        on_device,
        mesh=mesh,
        in_specs=(P("pgroup", "band", None), P("band", None), P("band", None), P("band")),
        out_specs=P("pgroup", "band", None),
        check_vma=False,
    )
```

```python
import functools

import jax
import jax.numpy as jnp
from jax import lax
from jax.experimental import pallas as pl
from jax.experimental.pallas import tpu as pltpu
from jax.sharding import PartitionSpec as P

PATCH_ROWS = 4
STEPS = 6
CAP = 2
LANES = 128
TILE = 8
VMEM = 56 << 20
SCALE = 0.05
MESH = pl.DeviceIdType.MESH
f32 = jnp.float32


def cut(low, high, most=TILE):
    pieces = -(-(high - low) // most)
    marks = [low + (high - low) * i // pieces for i in range(pieces + 1)]
    return [(a, b - a) for a, b in zip(marks[:-1], marks[1:])]


def split(value):
    return [value[..., b * LANES : (b + 1) * LANES] for b in range(value.shape[-1] // LANES)]


def kernel(
    bands, groups, chunks, state, forcing, parents, taper, out,
    st, done, fo, par, kinds, table, lookup, first, field, mixed, drive, weight, deal, undo,
    s_lo, s_hi, f_lo, f_hi, t_lo, t_hi, send,
    in_sem, halo_send, halo_recv, send_sem, recv_sem, *recvs,
):
    band, me = lax.axis_index("band"), lax.axis_index("pgroup")
    per_dev, tiles, blocks = state.shape[:3]
    extent, packs = tiles * TILE, per_dev // TILE
    patches = par.shape[0]
    quarter = tiles // 4
    has_low, has_high = band > 0, band < bands - 1
    up, down = lax.rem(band + 1, bands), lax.rem(band + bands - 1, bands)

    barrier = pltpu.get_barrier_semaphore()
    for step in range(1, groups):
        pl.semaphore_signal(
            barrier, inc=1, device_id={"pgroup": lax.rem(me + step, groups)}, device_id_type=MESH
        )

    @pl.when(has_low)
    def _():
        pl.semaphore_signal(barrier, inc=1, device_id={"band": down}, device_id_type=MESH)

    @pl.when(has_high)
    def _():
        pl.semaphore_signal(barrier, inc=1, device_id={"band": up}, device_id_type=MESH)

    def fetch(index, low, high):
        return pltpu.make_async_copy(
            state.at[:, low:high], st.at[:, low:high], in_sem.at[index]
        )

    inputs = [
        fetch(0, 2 * quarter - 2, 2 * quarter + 1),
        fetch(1, 0, 2 * quarter - 2),
        fetch(2, 2 * quarter + 1, tiles),
        pltpu.make_async_copy(forcing, fo, in_sem.at[3]),
        pltpu.make_async_copy(parents, par, in_sem.at[4]),
    ]
    for index in (0, 4, 3, 1, 2):
        inputs[index].start()

    def halo(index, src, low, high, last, start):
        upward = pltpu.make_async_remote_copy(
            src_ref=src.at[last], dst_ref=low,
            send_sem=halo_send.at[2 * index], recv_sem=halo_recv.at[2 * index],
            device_id={"band": up}, device_id_type=MESH,
        )
        downward = pltpu.make_async_remote_copy(
            src_ref=src.at[start], dst_ref=high,
            send_sem=halo_send.at[2 * index + 1], recv_sem=halo_recv.at[2 * index + 1],
            device_id={"band": down}, device_id_type=MESH,
        )
        return upward, downward

    every = slice(None)
    bottom, top = slice(0, TILE), slice(extent - TILE, extent)
    edges = [
        halo(0, state, s_lo, s_hi, (every, slice(tiles - 1, tiles)), (every, slice(0, 1))),
        halo(1, forcing, f_lo, f_hi, (top,), (bottom,)),
        halo(2, kinds, t_lo, t_hi, (top,), (bottom,)),
    ]
    middle = halo(
        3, mixed, mixed.at[:, 0:TILE], mixed.at[:, extent + TILE : extent + 2 * TILE],
        (every, slice(extent, extent + TILE)), (every, slice(TILE, 2 * TILE)),
    )

    def fill_edges():
        @pl.when(jnp.logical_not(has_low))
        def _():
            for ref in (s_lo, f_lo, t_lo):
                ref[...] = jnp.zeros_like(ref)
            mixed[:, 0:TILE] = jnp.zeros((packs, TILE, TILE, blocks * LANES), f32)

        @pl.when(jnp.logical_not(has_high))
        def _():
            for ref in (s_hi, f_hi, t_hi):
                ref[...] = jnp.zeros_like(ref)
            mixed[:, extent + TILE : extent + 2 * TILE] = jnp.zeros(
                (packs, TILE, TILE, blocks * LANES), f32
            )

    lane = lax.broadcasted_iota(jnp.int32, (TILE, LANES), 1)
    run = LANES // blocks
    order = (lane % run) * blocks + lane // run

    def exchange(parts):
        parts = list(parts)
        span, count = LANES // 2, blocks // 2
        while count:
            near = (lane & span) == 0
            for j in range(blocks):
                if j & count:
                    continue
                a, b = parts[j], parts[j + count]
                parts[j] = jnp.where(near, a, pltpu.roll(b, span, 1))
                parts[j + count] = jnp.where(near, pltpu.roll(a, LANES - span, 1), b)
            span, count = span // 2, count // 2
        return parts

    def interleave(parts):
        return exchange([jnp.take_along_axis(part, order, axis=1) for part in parts])

    def fill_orders():
        width = blocks * LANES
        for half in range(width // LANES):
            rows = slice(half * LANES, (half + 1) * LANES)
            spot = lax.broadcasted_iota(jnp.int32, (LANES, width), 0) + half * LANES
            col = lax.broadcasted_iota(jnp.int32, (LANES, width), 1)
            there = jnp.where((spot % blocks) * LANES + spot // blocks == col, 1.0, 0.0)
            there = there.astype(jnp.bfloat16)
            deal[rows] = there
            deal[width + half * LANES : width + (half + 1) * LANES] = there

    def fill_returns():
        width = blocks * LANES
        for half in range(width // LANES):
            rows = slice(half * LANES, (half + 1) * LANES)
            spot = lax.broadcasted_iota(jnp.int32, (LANES, width), 0) + half * LANES
            col = lax.broadcasted_iota(jnp.int32, (LANES, width), 1)
            back = jnp.where((col % blocks) * LANES + col // blocks == spot, 1.0 / SCALE, 0.0)
            back = back.astype(jnp.bfloat16)
            undo[rows] = back
            undo[width + half * LANES : width + (half + 1) * LANES] = back

    def permute(value, matrix):
        high = value.astype(jnp.bfloat16)
        low = (value - high.astype(f32)).astype(jnp.bfloat16)
        return jnp.dot(
            jnp.concatenate([high, low], axis=1), matrix[...], preferred_element_type=f32
        )

    def tables():
        value = par[...]
        spot = lax.broadcasted_iota(jnp.int32, value.shape, 1) % per_dev
        owner, within = value // per_dev, value % per_dev
        mine = owner == me
        least = jnp.where(mine, within, per_dev - 1)
        most = jnp.where(mine, within, 0)
        reach = 1
        while reach < per_dev:
            least = jnp.minimum(least, pltpu.roll(least, value.shape[1] - reach, 1))
            most = jnp.maximum(most, pltpu.roll(most, value.shape[1] - reach, 1))
            reach *= 2
        rank = jnp.zeros_like(value)
        for reach in range(1, per_dev):
            ahead = pltpu.roll(value, value.shape[1] - reach, 1)
            behind = pltpu.roll(value, per_dev - reach, 1)
            other = jnp.where(spot + reach < per_dev, ahead, behind)
            below = (other // per_dev == owner) & (other < value)
            rank = jnp.where(below, 1, rank)
        table[0] = least
        table[1] = most
        table[2] = owner
        table[3] = rank

    def piece(low, mid, high, row):
        if row < 0:
            return low, row + TILE
        if row >= extent:
            return high, row - extent
        return mid, row

    sub = lax.broadcasted_iota(jnp.int32, (TILE, LANES), 0)

    def fill_kinds():
        for tile in range(tiles):
            value = jnp.zeros((TILE, LANES), f32)
            for r in range(TILE):
                value = jnp.where(sub == r, taper[tile * TILE + r].astype(f32), value)
            kinds[tile * TILE : (tile + 1) * TILE] = value

    def fill_drive(low, high):
        for tile in range(low, high):
            ref, at = piece(f_lo, fo, f_hi, tile * TILE)
            parts = interleave([SCALE * part for part in split(ref[at : at + TILE])])
            for b, part in enumerate(parts):
                for r in range(TILE):
                    drive[(tile + 1) * TILE + r, :, b * LANES : (b + 1) * LANES] = (
                        jnp.broadcast_to(part[r : r + 1], (TILE, LANES))
                    )

    def fill_weight(low, high):
        for row in range(low, high):
            ref, at = piece(t_lo, kinds, t_hi, row)
            kind = jnp.broadcast_to(ref[pl.ds(at, 1), :], (TILE, LANES)) + 1.0
            near, far = jnp.exp(-0.2 * kind), jnp.exp(-0.8 * kind)
            scale = 1.0 / (1.0 + 2.0 * near + 2.0 * far)
            weight[0, row + TILE] = scale
            weight[1, row + TILE] = near * scale
            weight[2, row + TILE] = far * scale

    def clear(ref, low, high):
        if low < 0:
            ref[:, TILE - 1] = jnp.where(has_low, ref[:, TILE - 1], 0.0)
        if high > extent:
            ref[:, TILE + extent] = jnp.where(has_high, ref[:, TILE + extent], 0.0)

    def bounds(job, step):
        low, high, left, right = job
        rest = STEPS - step
        return low + (rest if left else -rest), high - (rest if right else -rest)

    def advance(source, target, pack, at, size):
        c = split(source[pack, at : at + size])
        n = split(source[pack, at + 1 : at + size + 1])
        s = split(source[pack, at - 1 : at + size - 1])
        d = split(drive[at : at + size])
        wrap_e = pltpu.roll(c[0], LANES - 1, 2)
        wrap_w = pltpu.roll(c[-1], 1, 2)
        for b in range(blocks):
            e = c[b + 1] if b < blocks - 1 else wrap_e
            w = c[b - 1] if b else wrap_w
            target[pack, at : at + size, :, b * LANES : (b + 1) * LANES] = (
                c[b] * (0.4 - (e - w)) + 0.15 * (e + w)
            ) + ((0.05 * n[b] + 0.25 * s[b]) + d[b])

    def sweep(job):
        for step in range(1, STEPS + 1):
            low, high = bounds(job, step)
            source, target = field.at[(step - 1) % 2], field.at[step % 2]
            for row, size in cut(low, high):
                for pack in range(packs):
                    advance(source, target, pack, row + TILE, size)
            if step < STEPS:
                clear(target, low, high)

    def load(low, high):
        if low >= high:
            return
        values = []
        for tile in range(low, high):
            if tile < 0:
                ref, at = s_lo, 0
            elif tile >= tiles:
                ref, at = s_hi, 0
            else:
                ref, at = st, tile
            for pack in range(packs):
                parts = [
                    jnp.swapaxes(ref[pack * TILE : (pack + 1) * TILE, at, b], 0, 1)
                    for b in range(blocks)
                ]
                values.append(
                    SCALE * jnp.concatenate(parts, axis=2).reshape(TILE * TILE, blocks * LANES)
                )
        result = permute(jnp.concatenate(values, axis=0), deal)
        at = 0
        for tile in range(low, high):
            for pack in range(packs):
                field[0, pack, (tile + 1) * TILE : (tile + 2) * TILE] = result[
                    at : at + TILE * TILE
                ].reshape(TILE, TILE, blocks * LANES)
                at += TILE * TILE

    upper = lax.broadcasted_iota(jnp.int32, (blocks, TILE, LANES), 1) < PATCH_ROWS

    def gather(index):
        base, count = chunks[index]
        for tile in range(base, base + count):
            for pack in range(packs):
                for b, part in enumerate(
                    split(field[0, pack, (tile + 1) * TILE : (tile + 2) * TILE])
                ):
                    first[pack * TILE : (pack + 1) * TILE, tile, b] = jnp.swapaxes(part, 0, 1)
        for tile in range(base, base + count):

            def body(g, carry, tile=tile):
                for slot in range(CAP):
                    even = lookup[slot, 2 * tile, g * per_dev]
                    odd = lookup[slot, 2 * tile + 1, g * per_dev]
                    send[g, tile, slot] = jnp.where(upper, first[even, tile], first[odd, tile])
                return carry

            lax.fori_loop(0, groups, body, 0)

    def scatter(index):
        base, count = chunks[index]
        recv = recvs[index]
        for tile in range(base, base + count):
            j = tile - base
            for pack in range(packs):
                children = []
                for k in range(pack * TILE, (pack + 1) * TILE):
                    at = me * per_dev + k
                    even = recv[lookup[2, 2 * tile, at], j, lookup[3, 2 * tile, at]]
                    odd = recv[lookup[2, 2 * tile + 1, at], j, lookup[3, 2 * tile + 1, at]]
                    children.append(jnp.where(upper, even, odd))
                for b in range(blocks):
                    mixed[
                        pack, (tile + 1) * TILE : (tile + 2) * TILE, :,
                        b * LANES : (b + 1) * LANES,
                    ] = jnp.swapaxes(jnp.stack([child[b] for child in children]), 0, 1)

    def blend(job):
        low, high = bounds(job, 0)
        for row, size in cut(low, high):
            at = row + TILE
            w = [weight[j, at : at + size] for j in range(3)]
            for pack in range(packs):
                near = [split(mixed[pack, at + j : at + j + size]) for j in range(-2, 3)]
                for b in range(blocks):
                    field[0, pack, at : at + size, :, b * LANES : (b + 1) * LANES] = (
                        w[0] * near[2][b]
                        + w[1] * (near[1][b] + near[3][b])
                        + w[2] * (near[0][b] + near[4][b])
                    )
        clear(field.at[0], low, high)

    def leave(low, high):
        return pltpu.make_async_copy(done.at[:, low:high], out.at[:, low:high], in_sem.at[6])

    def finish(low, high):
        values = [
            field[0, pack, (tile + 1) * TILE : (tile + 2) * TILE].reshape(
                TILE * TILE, blocks * LANES
            )
            for tile in range(low, high)
            for pack in range(packs)
        ]
        result = permute(jnp.concatenate(values, axis=0), undo)
        at = 0
        for tile in range(low, high):
            for pack in range(packs):
                parts = split(
                    result[at : at + TILE * TILE].reshape(TILE, TILE, blocks * LANES)
                )
                for b, part in enumerate(parts):
                    done[pack * TILE : (pack + 1) * TILE, tile, b] = jnp.swapaxes(part, 0, 1)
                at += TILE * TILE
        leave(low, high).start()

    shifts = sorted(range(1, groups), key=lambda i: -min(i, groups - i))

    def exchange_out(index):
        base, count = chunks[index]
        part = slice(base, base + count)
        for shift in shifts:
            to = lax.rem(me + shift, groups)
            pltpu.make_async_remote_copy(
                src_ref=send.at[to, part], dst_ref=recvs[index].at[me],
                send_sem=send_sem.at[0], recv_sem=recv_sem.at[index],
                device_id={"pgroup": to}, device_id_type=MESH,
            ).start()
        pltpu.make_async_copy(
            send.at[me, part], recvs[index].at[me], recv_sem.at[index]
        ).start()

    def exchange_in(index):
        base, count = chunks[index]
        part = slice(base, base + count)
        pltpu.make_async_copy(send.at[:, part], recvs[index], recv_sem.at[index]).wait()

    q = quarter
    fill_orders()
    inputs[4].wait()
    tables()
    to_lookup = pltpu.make_async_copy(table, lookup, in_sem.at[5])
    to_lookup.start()
    inputs[3].wait()
    fill_drive(2 * q - 2, 2 * q + 1)
    inputs[0].wait()
    load(2 * q - 2, 2 * q + 1)
    sweep((TILE * (2 * q - 1), TILE * 2 * q, False, False))
    to_lookup.wait()
    gather(0)
    pl.semaphore_wait(
        barrier, groups - 1 + has_low.astype(jnp.int32) + has_high.astype(jnp.int32)
    )
    exchange_out(0)
    fill_kinds()

    @pl.when(has_high)
    def _():
        for upward, _ in edges:
            upward.start()

    @pl.when(has_low)
    def _():
        for _, downward in edges:
            downward.start()

    fill_edges()
    inputs[1].wait()
    fill_drive(0, 2 * q - 2)
    load(q - 1, 2 * q - 2)
    sweep((TILE * q, TILE * (2 * q - 1), False, True))
    gather(1)
    exchange_out(1)
    inputs[2].wait()
    fill_drive(2 * q + 1, tiles)

    @pl.when(has_low)
    def _():
        for upward, _ in edges:
            upward.wait_recv()

    @pl.when(has_high)
    def _():
        for _, downward in edges:
            downward.wait_recv()

    fill_drive(-1, 0)
    fill_drive(tiles, tiles + 1)
    load(-1, q - 1)
    sweep((0, TILE * q, False, True))
    gather(2)
    exchange_out(2)
    load(3 * q - 1, tiles + 1)
    sweep((TILE * 3 * q, extent, False, False))
    gather(3)
    exchange_out(3)
    load(2 * q + 1, 3 * q - 1)
    sweep((TILE * 2 * q, TILE * 3 * q, True, True))
    gather(4)
    exchange_out(4)
    gather(5)
    exchange_out(5)
    fill_weight(-TILE, extent + TILE)
    fill_returns()

    def second(job):
        blend(job)
        sweep(job)
        finish(job[0] // TILE, job[1] // TILE)

    for index in range(3):
        exchange_in(index)
        scatter(index)

    @pl.when(has_low)
    def _():
        middle[1].start()

    second((TILE, TILE * (2 * q - 1), False, False))
    exchange_in(3)
    scatter(3)

    @pl.when(has_high)
    def _():
        middle[0].start()

    @pl.when(has_high)
    def _():
        middle[1].wait_recv()

    second((TILE * (3 * q + 1), extent, False, False))
    exchange_in(4)
    scatter(4)
    second((TILE * (2 * q - 1), TILE * (3 * q - 2), True, False))

    @pl.when(has_low)
    def _():
        middle[0].wait_recv()

    second((0, TILE, False, True))
    exchange_in(5)
    scatter(5)
    second((TILE * (3 * q - 2), TILE * (3 * q + 1), True, True))

    leave(0, tiles).wait()

    @pl.when(has_high)
    def _():
        for upward, _ in edges:
            upward.wait_send()
        middle[0].wait_send()

    @pl.when(has_low)
    def _():
        for _, downward in edges:
            downward.wait_send()
        middle[1].wait_send()

    sent = slice(0, groups - 1)
    pltpu.make_async_remote_copy(
        src_ref=send.at[sent], dst_ref=send.at[sent],
        send_sem=send_sem.at[0], recv_sem=recv_sem.at[0],
        device_id={"pgroup": lax.rem(me + 1, groups)}, device_id_type=MESH,
    ).wait_send()


def settle(value):
    pieces = 8
    size = value.shape[0] // pieces

    def kernel(source, target, held, in_sem, out_sem):
        parts = [pl.ds(i * size, size) for i in range(pieces)]
        ins = [
            pltpu.make_async_copy(source.at[part], held.at[part], in_sem.at[i])
            for i, part in enumerate(parts)
        ]
        for copy in ins:
            copy.start()
        for copy, part in zip(ins, parts):
            copy.wait()
            pltpu.make_async_copy(held.at[part], target.at[part], out_sem).start()
        pltpu.make_async_copy(held, target, out_sem).wait()

    hbm = pl.BlockSpec(memory_space=pltpu.HBM)
    return pl.pallas_call(
        kernel,
        out_shape=jax.ShapeDtypeStruct(value.shape, value.dtype),
        in_specs=[hbm],
        out_specs=hbm,
        scratch_shapes=[
            pltpu.VMEM(value.shape, value.dtype),
            pltpu.SemaphoreType.DMA((pieces,)),
            pltpu.SemaphoreType.DMA,
        ],
        compiler_params=pltpu.CompilerParams(vmem_limit_bytes=VMEM),
        name="settle",
    )(value)


def on_device(state, forcing, parents, taper_index):
    per_dev, extent, width = state.shape
    bands, groups = lax.axis_size("band"), lax.axis_size("pgroup")
    blocks, tiles, packs = width // LANES, extent // TILE, per_dev // TILE
    state = state.reshape(per_dev, tiles, TILE, blocks, LANES).transpose(0, 1, 3, 2, 4)
    q = tiles // 4
    chunks = [
        (2 * q - 1, 1),
        (q, q - 1),
        (0, q),
        (3 * q, q),
        (2 * q, q - 1),
        (3 * q - 1, 1),
    ]
    rows = extent + 2 * TILE
    edge = (per_dev, 1, blocks, TILE, LANES)
    slot = (CAP, blocks, TILE, LANES)
    smem, hbm = pl.BlockSpec(memory_space=pltpu.SMEM), pl.BlockSpec(memory_space=pltpu.HBM)
    out = pl.pallas_call(
        functools.partial(kernel, bands, groups, chunks),
        out_shape=jax.ShapeDtypeStruct(state.shape, f32),
        in_specs=[hbm, hbm, hbm, smem],
        out_specs=hbm,
        scratch_shapes=[
            pltpu.VMEM(state.shape, f32),
            pltpu.VMEM(state.shape, f32),
            pltpu.VMEM(forcing.shape, f32),
            pltpu.VMEM(parents.shape, jnp.int32),
            pltpu.VMEM((extent, LANES), f32),
            pltpu.VMEM((4, *parents.shape), jnp.int32),
            pltpu.SMEM((4, *parents.shape), jnp.int32),
            pltpu.VMEM(state.shape, f32),
            pltpu.VMEM((2, packs, rows, TILE, width), f32),
            pltpu.VMEM((packs, rows, TILE, width), f32),
            pltpu.VMEM((rows, TILE, width), f32),
            pltpu.VMEM((3, rows, TILE, LANES), f32),
            pltpu.VMEM((2 * width, width), jnp.bfloat16),
            pltpu.VMEM((2 * width, width), jnp.bfloat16),
            pltpu.VMEM(edge, f32),
            pltpu.VMEM(edge, f32),
            pltpu.VMEM((TILE, width), f32),
            pltpu.VMEM((TILE, width), f32),
            pltpu.VMEM((TILE, LANES), f32),
            pltpu.VMEM((TILE, LANES), f32),
            pltpu.VMEM((groups, tiles, *slot), f32),
            pltpu.SemaphoreType.DMA((7,)),
            pltpu.SemaphoreType.DMA((8,)),
            pltpu.SemaphoreType.DMA((8,)),
            pltpu.SemaphoreType.DMA((1,)),
            pltpu.SemaphoreType.DMA((len(chunks),)),
            *[pltpu.VMEM((groups, count, *slot), f32) for _, count in chunks],
        ],
        compiler_params=pltpu.CompilerParams(
            collective_id=0, has_side_effects=True, vmem_limit_bytes=VMEM
        ),
        name="filter_step",
    )(state, forcing, parents, taper_index)
    out = settle(out)
    return out.transpose(0, 1, 3, 2, 4).reshape(per_dev, extent, width)


def solution(mesh):
    return jax.shard_map(
        on_device,
        mesh=mesh,
        in_specs=(P("pgroup", "band", None), P("band", None), P("band", None), P("band")),
        out_specs=P("pgroup", "band", None),
        check_vma=False,
    )
```

```python
import functools

import jax
import jax.numpy as jnp
from jax import lax
from jax.experimental import pallas as pl
from jax.experimental.pallas import tpu as pltpu
from jax.sharding import PartitionSpec as P

PATCH_ROWS = 4
STEPS = 6
CAP = 2
LANES = 128
TILE = 8
VMEM = 56 << 20
SCALE = 0.05
MESH = pl.DeviceIdType.MESH
f32 = jnp.float32


def cut(low, high, most=TILE):
    pieces = -(-(high - low) // most)
    marks = [low + (high - low) * i // pieces for i in range(pieces + 1)]
    return [(a, b - a) for a, b in zip(marks[:-1], marks[1:])]


def split(value):
    return [value[..., b * LANES : (b + 1) * LANES] for b in range(value.shape[-1] // LANES)]


def kernel(
    bands, groups, chunks, state, forcing, parents, taper_index, out,
    st, done, fo, par, taper, kinds, table, lookup, first, field, mixed, drive, weight, deal, undo,
    s_lo, s_hi, f_lo, f_hi, t_lo, t_hi, send,
    in_sem, halo_send, halo_recv, send_sem, recv_sem, *recvs,
):
    band, me = lax.axis_index("band"), lax.axis_index("pgroup")
    per_dev, tiles, blocks = state.shape[:3]
    extent, packs = tiles * TILE, per_dev // TILE
    patches = par.shape[0]
    quarter = tiles // 4
    has_low, has_high = band > 0, band < bands - 1
    up, down = lax.rem(band + 1, bands), lax.rem(band + bands - 1, bands)

    barrier = pltpu.get_barrier_semaphore()
    for step in range(1, groups):
        pl.semaphore_signal(
            barrier, inc=1, device_id={"pgroup": lax.rem(me + step, groups)}, device_id_type=MESH
        )

    @pl.when(has_low)
    def _():
        pl.semaphore_signal(barrier, inc=1, device_id={"band": down}, device_id_type=MESH)

    @pl.when(has_high)
    def _():
        pl.semaphore_signal(barrier, inc=1, device_id={"band": up}, device_id_type=MESH)

    def fetch(index, low, high):
        return pltpu.make_async_copy(
            state.at[:, low:high], st.at[:, low:high], in_sem.at[index]
        )

    inputs = [
        fetch(0, 2 * quarter - 2, 2 * quarter + 1),
        fetch(1, 0, 2 * quarter - 2),
        fetch(2, 2 * quarter + 1, tiles),
        pltpu.make_async_copy(forcing, fo, in_sem.at[3]),
        pltpu.make_async_copy(parents, par, in_sem.at[4]),
        pltpu.make_async_copy(taper_index, taper, in_sem.at[7]),
    ]
    for index in (4, 0, 3, 5, 1, 2):
        inputs[index].start()

    def halo(index, src, low, high, last, start):
        upward = pltpu.make_async_remote_copy(
            src_ref=src.at[last], dst_ref=low,
            send_sem=halo_send.at[2 * index], recv_sem=halo_recv.at[2 * index],
            device_id={"band": up}, device_id_type=MESH,
        )
        downward = pltpu.make_async_remote_copy(
            src_ref=src.at[start], dst_ref=high,
            send_sem=halo_send.at[2 * index + 1], recv_sem=halo_recv.at[2 * index + 1],
            device_id={"band": down}, device_id_type=MESH,
        )
        return upward, downward

    every = slice(None)
    bottom, top = slice(0, TILE), slice(extent - TILE, extent)
    edges = [
        halo(0, state, s_lo, s_hi, (every, slice(tiles - 1, tiles)), (every, slice(0, 1))),
        halo(1, forcing, f_lo, f_hi, (top,), (bottom,)),
        halo(2, kinds, t_lo, t_hi, (top,), (bottom,)),
    ]
    middle = halo(
        3, mixed, mixed.at[:, 0:TILE], mixed.at[:, extent + TILE : extent + 2 * TILE],
        (every, slice(extent, extent + TILE)), (every, slice(TILE, 2 * TILE)),
    )

    def fill_edges():
        @pl.when(jnp.logical_not(has_low))
        def _():
            for ref in (s_lo, f_lo, t_lo):
                ref[...] = jnp.zeros_like(ref)
            mixed[:, 0:TILE] = jnp.zeros((packs, TILE, TILE, blocks * LANES), f32)

        @pl.when(jnp.logical_not(has_high))
        def _():
            for ref in (s_hi, f_hi, t_hi):
                ref[...] = jnp.zeros_like(ref)
            mixed[:, extent + TILE : extent + 2 * TILE] = jnp.zeros(
                (packs, TILE, TILE, blocks * LANES), f32
            )

    lane = lax.broadcasted_iota(jnp.int32, (TILE, LANES), 1)
    run = LANES // blocks
    order = (lane % run) * blocks + lane // run

    def exchange(parts):
        parts = list(parts)
        span, count = LANES // 2, blocks // 2
        while count:
            near = (lane & span) == 0
            for j in range(blocks):
                if j & count:
                    continue
                a, b = parts[j], parts[j + count]
                parts[j] = jnp.where(near, a, pltpu.roll(b, span, 1))
                parts[j + count] = jnp.where(near, pltpu.roll(a, LANES - span, 1), b)
            span, count = span // 2, count // 2
        return parts

    def interleave(parts):
        return exchange([jnp.take_along_axis(part, order, axis=1) for part in parts])

    def fill_orders():
        width = blocks * LANES
        for half in range(width // LANES):
            rows = slice(half * LANES, (half + 1) * LANES)
            spot = lax.broadcasted_iota(jnp.int32, (LANES, width), 0) + half * LANES
            col = lax.broadcasted_iota(jnp.int32, (LANES, width), 1)
            there = jnp.where((spot % blocks) * LANES + spot // blocks == col, 1.0, 0.0)
            there = there.astype(jnp.bfloat16)
            deal[rows] = there
            deal[width + half * LANES : width + (half + 1) * LANES] = there

    def fill_returns():
        width = blocks * LANES
        for half in range(width // LANES):
            rows = slice(half * LANES, (half + 1) * LANES)
            spot = lax.broadcasted_iota(jnp.int32, (LANES, width), 0) + half * LANES
            col = lax.broadcasted_iota(jnp.int32, (LANES, width), 1)
            back = jnp.where((col % blocks) * LANES + col // blocks == spot, 1.0 / SCALE, 0.0)
            back = back.astype(jnp.bfloat16)
            undo[rows] = back
            undo[width + half * LANES : width + (half + 1) * LANES] = back

    def permute(value, matrix):
        high = value.astype(jnp.bfloat16)
        low = (value - high.astype(f32)).astype(jnp.bfloat16)
        return jnp.dot(
            jnp.concatenate([high, low], axis=1), matrix[...], preferred_element_type=f32
        )

    def tables():
        value = par[...]
        spot = lax.broadcasted_iota(jnp.int32, value.shape, 1) % per_dev
        owner, within = value // per_dev, value % per_dev
        mine = owner == me
        least = jnp.where(mine, within, per_dev - 1)
        most = jnp.where(mine, within, 0)
        reach = 1
        while reach < per_dev:
            least = jnp.minimum(least, pltpu.roll(least, value.shape[1] - reach, 1))
            most = jnp.maximum(most, pltpu.roll(most, value.shape[1] - reach, 1))
            reach *= 2
        rank = jnp.zeros_like(value)
        for reach in range(1, per_dev):
            ahead = pltpu.roll(value, value.shape[1] - reach, 1)
            behind = pltpu.roll(value, per_dev - reach, 1)
            other = jnp.where(spot + reach < per_dev, ahead, behind)
            below = (other // per_dev == owner) & (other < value)
            rank = jnp.where(below, 1, rank)
        table[0] = least
        table[1] = most
        table[2] = owner
        table[3] = rank

    def piece(low, mid, high, row):
        if row < 0:
            return low, row + TILE
        if row >= extent:
            return high, row - extent
        return mid, row

    sub = lax.broadcasted_iota(jnp.int32, (TILE, LANES), 0)

    def fill_kinds():
        for tile in range(tiles):
            value = jnp.zeros((TILE, LANES), f32)
            for r in range(TILE):
                value = jnp.where(sub == r, taper[tile * TILE + r].astype(f32), value)
            kinds[tile * TILE : (tile + 1) * TILE] = value

    def fill_drive(low, high):
        for tile in range(low, high):
            ref, at = piece(f_lo, fo, f_hi, tile * TILE)
            parts = interleave([SCALE * part for part in split(ref[at : at + TILE])])
            for b, part in enumerate(parts):
                for r in range(TILE):
                    drive[(tile + 1) * TILE + r, :, b * LANES : (b + 1) * LANES] = (
                        jnp.broadcast_to(part[r : r + 1], (TILE, LANES))
                    )

    def fill_weight(low, high):
        for row in range(low, high):
            ref, at = piece(t_lo, kinds, t_hi, row)
            kind = jnp.broadcast_to(ref[pl.ds(at, 1), :], (TILE, LANES)) + 1.0
            near, far = jnp.exp(-0.2 * kind), jnp.exp(-0.8 * kind)
            scale = 1.0 / (1.0 + 2.0 * near + 2.0 * far)
            weight[0, row + TILE] = scale
            weight[1, row + TILE] = near * scale
            weight[2, row + TILE] = far * scale

    def clear(ref, low, high):
        if low < 0:
            ref[:, TILE - 1] = jnp.where(has_low, ref[:, TILE - 1], 0.0)
        if high > extent:
            ref[:, TILE + extent] = jnp.where(has_high, ref[:, TILE + extent], 0.0)

    def bounds(job, step):
        low, high, left, right = job
        rest = STEPS - step
        return low + (rest if left else -rest), high - (rest if right else -rest)

    def advance(source, target, pack, at, size):
        c = split(source[pack, at : at + size])
        n = split(source[pack, at + 1 : at + size + 1])
        s = split(source[pack, at - 1 : at + size - 1])
        d = split(drive[at : at + size])
        wrap_e = pltpu.roll(c[0], LANES - 1, 2)
        wrap_w = pltpu.roll(c[-1], 1, 2)
        for b in range(blocks):
            e = c[b + 1] if b < blocks - 1 else wrap_e
            w = c[b - 1] if b else wrap_w
            target[pack, at : at + size, :, b * LANES : (b + 1) * LANES] = (
                c[b] * (0.4 - (e - w)) + 0.15 * (e + w)
            ) + ((0.05 * n[b] + 0.25 * s[b]) + d[b])

    def sweep(job):
        for step in range(1, STEPS + 1):
            low, high = bounds(job, step)
            source, target = field.at[(step - 1) % 2], field.at[step % 2]
            for row, size in cut(low, high):
                for pack in range(packs):
                    advance(source, target, pack, row + TILE, size)
            if step < STEPS:
                clear(target, low, high)

    def load(low, high):
        if low >= high:
            return
        values = []
        for tile in range(low, high):
            if tile < 0:
                ref, at = s_lo, 0
            elif tile >= tiles:
                ref, at = s_hi, 0
            else:
                ref, at = st, tile
            for pack in range(packs):
                parts = [
                    jnp.swapaxes(ref[pack * TILE : (pack + 1) * TILE, at, b], 0, 1)
                    for b in range(blocks)
                ]
                values.append(
                    SCALE * jnp.concatenate(parts, axis=2).reshape(TILE * TILE, blocks * LANES)
                )
        result = permute(jnp.concatenate(values, axis=0), deal)
        at = 0
        for tile in range(low, high):
            for pack in range(packs):
                field[0, pack, (tile + 1) * TILE : (tile + 2) * TILE] = result[
                    at : at + TILE * TILE
                ].reshape(TILE, TILE, blocks * LANES)
                at += TILE * TILE

    upper = lax.broadcasted_iota(jnp.int32, (blocks, TILE, LANES), 1) < PATCH_ROWS

    def gather(index):
        base, count = chunks[index]
        for tile in range(base, base + count):
            for pack in range(packs):
                for b, part in enumerate(
                    split(field[0, pack, (tile + 1) * TILE : (tile + 2) * TILE])
                ):
                    first[pack * TILE : (pack + 1) * TILE, tile, b] = jnp.swapaxes(part, 0, 1)
        for tile in range(base, base + count):

            def body(g, carry, tile=tile):
                for slot in range(CAP):
                    even = lookup[slot, 2 * tile, g * per_dev]
                    odd = lookup[slot, 2 * tile + 1, g * per_dev]
                    send[g, tile, slot] = jnp.where(upper, first[even, tile], first[odd, tile])
                return carry

            lax.fori_loop(0, groups, body, 0)

    def scatter(index):
        base, count = chunks[index]
        recv = recvs[index]
        for tile in range(base, base + count):
            j = tile - base
            for pack in range(packs):
                children = []
                for k in range(pack * TILE, (pack + 1) * TILE):
                    at = me * per_dev + k
                    even = recv[lookup[2, 2 * tile, at], j, lookup[3, 2 * tile, at]]
                    odd = recv[lookup[2, 2 * tile + 1, at], j, lookup[3, 2 * tile + 1, at]]
                    children.append(jnp.where(upper, even, odd))
                for b in range(blocks):
                    mixed[
                        pack, (tile + 1) * TILE : (tile + 2) * TILE, :,
                        b * LANES : (b + 1) * LANES,
                    ] = jnp.swapaxes(jnp.stack([child[b] for child in children]), 0, 1)

    def blend(job):
        low, high = bounds(job, 0)
        for row, size in cut(low, high):
            at = row + TILE
            w = [weight[j, at : at + size] for j in range(3)]
            for pack in range(packs):
                near = [split(mixed[pack, at + j : at + j + size]) for j in range(-2, 3)]
                for b in range(blocks):
                    field[0, pack, at : at + size, :, b * LANES : (b + 1) * LANES] = (
                        w[0] * near[2][b]
                        + w[1] * (near[1][b] + near[3][b])
                        + w[2] * (near[0][b] + near[4][b])
                    )
        clear(field.at[0], low, high)

    def leave(low, high):
        return pltpu.make_async_copy(done.at[:, low:high], out.at[:, low:high], in_sem.at[6])

    def finish(low, high):
        values = [
            field[0, pack, (tile + 1) * TILE : (tile + 2) * TILE].reshape(
                TILE * TILE, blocks * LANES
            )
            for tile in range(low, high)
            for pack in range(packs)
        ]
        result = permute(jnp.concatenate(values, axis=0), undo)
        at = 0
        for tile in range(low, high):
            for pack in range(packs):
                parts = split(
                    result[at : at + TILE * TILE].reshape(TILE, TILE, blocks * LANES)
                )
                for b, part in enumerate(parts):
                    done[pack * TILE : (pack + 1) * TILE, tile, b] = jnp.swapaxes(part, 0, 1)
                at += TILE * TILE
        leave(low, high).start()

    shifts = sorted(range(1, groups), key=lambda i: -min(i, groups - i))

    def exchange_out(index):
        base, count = chunks[index]
        part = slice(base, base + count)
        for shift in shifts:
            to = lax.rem(me + shift, groups)
            pltpu.make_async_remote_copy(
                src_ref=send.at[to, part], dst_ref=recvs[index].at[me],
                send_sem=send_sem.at[0], recv_sem=recv_sem.at[index],
                device_id={"pgroup": to}, device_id_type=MESH,
            ).start()
        pltpu.make_async_copy(
            send.at[me, part], recvs[index].at[me], recv_sem.at[index]
        ).start()

    def exchange_in(index):
        base, count = chunks[index]
        part = slice(base, base + count)
        pltpu.make_async_copy(send.at[:, part], recvs[index], recv_sem.at[index]).wait()

    q = quarter
    fill_orders()
    inputs[4].wait()
    tables()
    to_lookup = pltpu.make_async_copy(table, lookup, in_sem.at[5])
    to_lookup.start()
    inputs[3].wait()
    fill_drive(2 * q - 2, 2 * q + 1)
    inputs[0].wait()
    load(2 * q - 2, 2 * q + 1)
    sweep((TILE * (2 * q - 1), TILE * 2 * q, False, False))
    to_lookup.wait()
    gather(0)
    pl.semaphore_wait(
        barrier, groups - 1 + has_low.astype(jnp.int32) + has_high.astype(jnp.int32)
    )
    exchange_out(0)
    inputs[5].wait()
    fill_kinds()

    @pl.when(has_high)
    def _():
        for upward, _ in edges:
            upward.start()

    @pl.when(has_low)
    def _():
        for _, downward in edges:
            downward.start()

    fill_edges()
    inputs[1].wait()
    fill_drive(0, 2 * q - 2)
    load(q - 1, 2 * q - 2)
    sweep((TILE * q, TILE * (2 * q - 1), False, True))
    gather(1)
    exchange_out(1)
    inputs[2].wait()
    fill_drive(2 * q + 1, tiles)

    @pl.when(has_low)
    def _():
        for upward, _ in edges:
            upward.wait_recv()

    @pl.when(has_high)
    def _():
        for _, downward in edges:
            downward.wait_recv()

    fill_drive(-1, 0)
    fill_drive(tiles, tiles + 1)
    load(-1, q - 1)
    sweep((0, TILE * q, False, True))
    gather(2)
    exchange_out(2)
    load(3 * q - 1, tiles + 1)
    sweep((TILE * 3 * q, extent, False, False))
    gather(3)
    exchange_out(3)
    load(2 * q + 1, 3 * q - 1)
    sweep((TILE * 2 * q, TILE * 3 * q, True, True))
    gather(4)
    exchange_out(4)
    gather(5)
    exchange_out(5)
    fill_weight(-TILE, extent + TILE)
    fill_returns()

    def second(job):
        blend(job)
        sweep(job)
        finish(job[0] // TILE, job[1] // TILE)

    for index in range(3):
        exchange_in(index)
        scatter(index)

    @pl.when(has_low)
    def _():
        middle[1].start()

    second((TILE, TILE * (2 * q - 1), False, False))
    exchange_in(3)
    scatter(3)

    @pl.when(has_high)
    def _():
        middle[0].start()

    @pl.when(has_high)
    def _():
        middle[1].wait_recv()

    second((TILE * (3 * q + 1), extent, False, False))
    exchange_in(4)
    scatter(4)
    second((TILE * (2 * q - 1), TILE * (3 * q - 2), True, False))

    @pl.when(has_low)
    def _():
        middle[0].wait_recv()

    second((0, TILE, False, True))
    exchange_in(5)
    scatter(5)
    second((TILE * (3 * q - 2), TILE * (3 * q + 1), True, True))

    leave(0, tiles).wait()

    @pl.when(has_high)
    def _():
        for upward, _ in edges:
            upward.wait_send()
        middle[0].wait_send()

    @pl.when(has_low)
    def _():
        for _, downward in edges:
            downward.wait_send()
        middle[1].wait_send()

    sent = slice(0, groups - 1)
    pltpu.make_async_remote_copy(
        src_ref=send.at[sent], dst_ref=send.at[sent],
        send_sem=send_sem.at[0], recv_sem=recv_sem.at[0],
        device_id={"pgroup": lax.rem(me + 1, groups)}, device_id_type=MESH,
    ).wait_send()


def settle(value):
    pieces = 8
    size = value.shape[0] // pieces

    def kernel(source, target, held, in_sem, out_sem):
        parts = [pl.ds(i * size, size) for i in range(pieces)]
        ins = [
            pltpu.make_async_copy(source.at[part], held.at[part], in_sem.at[i])
            for i, part in enumerate(parts)
        ]
        for copy in ins:
            copy.start()
        for copy, part in zip(ins, parts):
            copy.wait()
            pltpu.make_async_copy(held.at[part], target.at[part], out_sem).start()
        pltpu.make_async_copy(held, target, out_sem).wait()

    hbm = pl.BlockSpec(memory_space=pltpu.HBM)
    return pl.pallas_call(
        kernel,
        out_shape=jax.ShapeDtypeStruct(value.shape, value.dtype),
        in_specs=[hbm],
        out_specs=hbm,
        scratch_shapes=[
            pltpu.VMEM(value.shape, value.dtype),
            pltpu.SemaphoreType.DMA((pieces,)),
            pltpu.SemaphoreType.DMA,
        ],
        compiler_params=pltpu.CompilerParams(vmem_limit_bytes=VMEM),
        name="settle",
    )(value)


def on_device(state, forcing, parents, taper_index):
    per_dev, extent, width = state.shape
    bands, groups = lax.axis_size("band"), lax.axis_size("pgroup")
    blocks, tiles, packs = width // LANES, extent // TILE, per_dev // TILE
    state = state.reshape(per_dev, tiles, TILE, blocks, LANES).transpose(0, 1, 3, 2, 4)
    q = tiles // 4
    chunks = [
        (2 * q - 1, 1),
        (q, q - 1),
        (0, q),
        (3 * q, q),
        (2 * q, q - 1),
        (3 * q - 1, 1),
    ]
    rows = extent + 2 * TILE
    edge = (per_dev, 1, blocks, TILE, LANES)
    slot = (CAP, blocks, TILE, LANES)
    hbm = pl.BlockSpec(memory_space=pltpu.HBM)
    out = pl.pallas_call(
        functools.partial(kernel, bands, groups, chunks),
        out_shape=jax.ShapeDtypeStruct(state.shape, f32),
        in_specs=[hbm, hbm, hbm, hbm],
        out_specs=hbm,
        scratch_shapes=[
            pltpu.VMEM(state.shape, f32),
            pltpu.VMEM(state.shape, f32),
            pltpu.VMEM(forcing.shape, f32),
            pltpu.VMEM(parents.shape, jnp.int32),
            pltpu.SMEM(taper_index.shape, jnp.int32),
            pltpu.VMEM((extent, LANES), f32),
            pltpu.VMEM((4, *parents.shape), jnp.int32),
            pltpu.SMEM((4, *parents.shape), jnp.int32),
            pltpu.VMEM(state.shape, f32),
            pltpu.VMEM((2, packs, rows, TILE, width), f32),
            pltpu.VMEM((packs, rows, TILE, width), f32),
            pltpu.VMEM((rows, TILE, width), f32),
            pltpu.VMEM((3, rows, TILE, LANES), f32),
            pltpu.VMEM((2 * width, width), jnp.bfloat16),
            pltpu.VMEM((2 * width, width), jnp.bfloat16),
            pltpu.VMEM(edge, f32),
            pltpu.VMEM(edge, f32),
            pltpu.VMEM((TILE, width), f32),
            pltpu.VMEM((TILE, width), f32),
            pltpu.VMEM((TILE, LANES), f32),
            pltpu.VMEM((TILE, LANES), f32),
            pltpu.VMEM((groups, tiles, *slot), f32),
            pltpu.SemaphoreType.DMA((8,)),
            pltpu.SemaphoreType.DMA((8,)),
            pltpu.SemaphoreType.DMA((8,)),
            pltpu.SemaphoreType.DMA((1,)),
            pltpu.SemaphoreType.DMA((len(chunks),)),
            *[pltpu.VMEM((groups, count, *slot), f32) for _, count in chunks],
        ],
        compiler_params=pltpu.CompilerParams(
            collective_id=0, has_side_effects=True, vmem_limit_bytes=VMEM
        ),
        name="filter_step",
    )(state, forcing, parents, taper_index)
    out = settle(out)
    return out.transpose(0, 1, 3, 2, 4).reshape(per_dev, extent, width)


def solution(mesh):
    return jax.shard_map(
        on_device,
        mesh=mesh,
        in_specs=(P("pgroup", "band", None), P("band", None), P("band", None), P("band")),
        out_specs=P("pgroup", "band", None),
        check_vma=False,
    )
```

```python
import functools

import jax
import jax.numpy as jnp
from jax import lax
from jax.experimental import pallas as pl
from jax.experimental.pallas import tpu as pltpu
from jax.sharding import PartitionSpec as P

PATCH_ROWS = 4
STEPS = 6
CAP = 2
LANES = 128
TILE = 8
VMEM = 56 << 20
SCALE = 0.05
MESH = pl.DeviceIdType.MESH
f32 = jnp.float32


def cut(low, high, most=TILE):
    pieces = -(-(high - low) // most)
    marks = [low + (high - low) * i // pieces for i in range(pieces + 1)]
    return [(a, b - a) for a, b in zip(marks[:-1], marks[1:])]


def split(value):
    return [value[..., b * LANES : (b + 1) * LANES] for b in range(value.shape[-1] // LANES)]


def kernel(
    bands, groups, chunks, state, forcing, parents, taper_index, out,
    st, done, fo, par, taper, kinds, table, lookup, first, field, mixed, drive, weight, deal, undo,
    s_lo, s_hi, f_lo, f_hi, t_lo, t_hi, send,
    in_sem, halo_send, halo_recv, send_sem, recv_sem, *recvs,
):
    band, me = lax.axis_index("band"), lax.axis_index("pgroup")
    per_dev, tiles, blocks = state.shape[:3]
    extent, packs = tiles * TILE, per_dev // TILE
    patches = par.shape[0]
    quarter = tiles // 4
    has_low, has_high = band > 0, band < bands - 1
    up, down = lax.rem(band + 1, bands), lax.rem(band + bands - 1, bands)

    barrier = pltpu.get_barrier_semaphore()
    for step in range(1, groups):
        pl.semaphore_signal(
            barrier, inc=1, device_id={"pgroup": lax.rem(me + step, groups)}, device_id_type=MESH
        )

    @pl.when(has_low)
    def _():
        pl.semaphore_signal(barrier, inc=1, device_id={"band": down}, device_id_type=MESH)

    @pl.when(has_high)
    def _():
        pl.semaphore_signal(barrier, inc=1, device_id={"band": up}, device_id_type=MESH)

    def fetch(index, low, high):
        return pltpu.make_async_copy(
            state.at[:, low:high], st.at[:, low:high], in_sem.at[index]
        )

    inputs = [
        fetch(0, 2 * quarter - 2, 2 * quarter + 1),
        fetch(1, 0, 2 * quarter - 2),
        fetch(2, 2 * quarter + 1, tiles),
        pltpu.make_async_copy(forcing, fo, in_sem.at[3]),
        pltpu.make_async_copy(parents, par, in_sem.at[4]),
        pltpu.make_async_copy(taper_index, taper, in_sem.at[7]),
    ]
    for index in (4, 0, 3, 5, 1, 2):
        inputs[index].start()

    def halo(index, src, low, high, last, start):
        upward = pltpu.make_async_remote_copy(
            src_ref=src.at[last], dst_ref=low,
            send_sem=halo_send.at[2 * index], recv_sem=halo_recv.at[2 * index],
            device_id={"band": up}, device_id_type=MESH,
        )
        downward = pltpu.make_async_remote_copy(
            src_ref=src.at[start], dst_ref=high,
            send_sem=halo_send.at[2 * index + 1], recv_sem=halo_recv.at[2 * index + 1],
            device_id={"band": down}, device_id_type=MESH,
        )
        return upward, downward

    every = slice(None)
    bottom, top = slice(0, TILE), slice(extent - TILE, extent)
    edges = [
        halo(0, state, s_lo, s_hi, (every, slice(tiles - 1, tiles)), (every, slice(0, 1))),
        halo(1, forcing, f_lo, f_hi, (top,), (bottom,)),
        halo(2, kinds, t_lo, t_hi, (top,), (bottom,)),
    ]
    middle = halo(
        3, mixed, mixed.at[:, 0:TILE], mixed.at[:, extent + TILE : extent + 2 * TILE],
        (every, slice(extent, extent + TILE)), (every, slice(TILE, 2 * TILE)),
    )

    def fill_edges():
        @pl.when(jnp.logical_not(has_low))
        def _():
            for ref in (s_lo, f_lo, t_lo):
                ref[...] = jnp.zeros_like(ref)
            mixed[:, 0:TILE] = jnp.zeros((packs, TILE, TILE, blocks * LANES), f32)

        @pl.when(jnp.logical_not(has_high))
        def _():
            for ref in (s_hi, f_hi, t_hi):
                ref[...] = jnp.zeros_like(ref)
            mixed[:, extent + TILE : extent + 2 * TILE] = jnp.zeros(
                (packs, TILE, TILE, blocks * LANES), f32
            )

    lane = lax.broadcasted_iota(jnp.int32, (TILE, LANES), 1)
    run = LANES // blocks
    order = (lane % run) * blocks + lane // run

    def exchange(parts):
        parts = list(parts)
        span, count = LANES // 2, blocks // 2
        while count:
            near = (lane & span) == 0
            for j in range(blocks):
                if j & count:
                    continue
                a, b = parts[j], parts[j + count]
                parts[j] = jnp.where(near, a, pltpu.roll(b, span, 1))
                parts[j + count] = jnp.where(near, pltpu.roll(a, LANES - span, 1), b)
            span, count = span // 2, count // 2
        return parts

    def interleave(parts):
        return exchange([jnp.take_along_axis(part, order, axis=1) for part in parts])

    def fill_orders():
        width = blocks * LANES
        for half in range(width // LANES):
            rows = slice(half * LANES, (half + 1) * LANES)
            spot = lax.broadcasted_iota(jnp.int32, (LANES, width), 0) + half * LANES
            col = lax.broadcasted_iota(jnp.int32, (LANES, width), 1)
            there = jnp.where((spot % blocks) * LANES + spot // blocks == col, 1.0, 0.0)
            there = there.astype(jnp.bfloat16)
            deal[rows] = there
            deal[width + half * LANES : width + (half + 1) * LANES] = there

    def fill_returns():
        width = blocks * LANES
        for half in range(width // LANES):
            rows = slice(half * LANES, (half + 1) * LANES)
            spot = lax.broadcasted_iota(jnp.int32, (LANES, width), 0) + half * LANES
            col = lax.broadcasted_iota(jnp.int32, (LANES, width), 1)
            back = jnp.where((col % blocks) * LANES + col // blocks == spot, 1.0 / SCALE, 0.0)
            back = back.astype(jnp.bfloat16)
            undo[rows] = back
            undo[width + half * LANES : width + (half + 1) * LANES] = back

    def permute(value, matrix):
        high = value.astype(jnp.bfloat16)
        low = (value - high.astype(f32)).astype(jnp.bfloat16)
        return jnp.dot(
            jnp.concatenate([high, low], axis=1), matrix[...], preferred_element_type=f32
        )

    def tables():
        value = par[...]
        spot = lax.broadcasted_iota(jnp.int32, value.shape, 1) % per_dev
        owner, within = value // per_dev, value % per_dev
        mine = owner == me
        least = jnp.where(mine, within, per_dev - 1)
        most = jnp.where(mine, within, 0)
        reach = 1
        while reach < per_dev:
            least = jnp.minimum(least, pltpu.roll(least, value.shape[1] - reach, 1))
            most = jnp.maximum(most, pltpu.roll(most, value.shape[1] - reach, 1))
            reach *= 2
        rank = jnp.zeros_like(value)
        for reach in range(1, per_dev):
            ahead = pltpu.roll(value, value.shape[1] - reach, 1)
            behind = pltpu.roll(value, per_dev - reach, 1)
            other = jnp.where(spot + reach < per_dev, ahead, behind)
            below = (other // per_dev == owner) & (other < value)
            rank = jnp.where(below, 1, rank)
        table[0] = least
        table[1] = most
        table[2] = owner
        table[3] = rank

    def piece(low, mid, high, row):
        if row < 0:
            return low, row + TILE
        if row >= extent:
            return high, row - extent
        return mid, row

    sub = lax.broadcasted_iota(jnp.int32, (TILE, LANES), 0)

    def fill_kinds():
        for tile in range(tiles):
            value = jnp.zeros((TILE, LANES), f32)
            for r in range(TILE):
                value = jnp.where(sub == r, taper[tile * TILE + r].astype(f32), value)
            kinds[tile * TILE : (tile + 1) * TILE] = value

    def fill_drive(low, high):
        for tile in range(low, high):
            ref, at = piece(f_lo, fo, f_hi, tile * TILE)
            parts = interleave([SCALE * part for part in split(ref[at : at + TILE])])
            for b, part in enumerate(parts):
                for r in range(TILE):
                    drive[(tile + 1) * TILE + r, :, b * LANES : (b + 1) * LANES] = (
                        jnp.broadcast_to(part[r : r + 1], (TILE, LANES))
                    )

    def fill_weight(low, high):
        for row in range(low, high):
            ref, at = piece(t_lo, kinds, t_hi, row)
            kind = jnp.broadcast_to(ref[pl.ds(at, 1), :], (TILE, LANES)) + 1.0
            near, far = jnp.exp(-0.2 * kind), jnp.exp(-0.8 * kind)
            scale = 1.0 / (1.0 + 2.0 * near + 2.0 * far)
            weight[0, row + TILE] = scale
            weight[1, row + TILE] = near * scale
            weight[2, row + TILE] = far * scale

    def clear(ref, low, high):
        if low < 0:
            ref[:, TILE - 1] = jnp.where(has_low, ref[:, TILE - 1], 0.0)
        if high > extent:
            ref[:, TILE + extent] = jnp.where(has_high, ref[:, TILE + extent], 0.0)

    def bounds(job, step):
        low, high, left, right = job
        rest = STEPS - step
        return low + (rest if left else -rest), high - (rest if right else -rest)

    def advance(source, target, pack, at, size):
        c = split(source[pack, at : at + size])
        n = split(source[pack, at + 1 : at + size + 1])
        s = split(source[pack, at - 1 : at + size - 1])
        d = split(drive[at : at + size])
        wrap_e = pltpu.roll(c[0], LANES - 1, 2)
        wrap_w = pltpu.roll(c[-1], 1, 2)
        for b in range(blocks):
            e = c[b + 1] if b < blocks - 1 else wrap_e
            w = c[b - 1] if b else wrap_w
            target[pack, at : at + size, :, b * LANES : (b + 1) * LANES] = (
                c[b] * (0.4 - (e - w)) + 0.15 * (e + w)
            ) + ((0.05 * n[b] + 0.25 * s[b]) + d[b])

    def sweep(job):
        for step in range(1, STEPS + 1):
            low, high = bounds(job, step)
            source, target = field.at[(step - 1) % 2], field.at[step % 2]
            for row, size in cut(low, high):
                for pack in range(packs):
                    advance(source, target, pack, row + TILE, size)
            if step < STEPS:
                clear(target, low, high)

    def load(low, high):
        if low >= high:
            return
        values = []
        for tile in range(low, high):
            if tile < 0:
                ref, at = s_lo, 0
            elif tile >= tiles:
                ref, at = s_hi, 0
            else:
                ref, at = st, tile
            for pack in range(packs):
                parts = [
                    jnp.swapaxes(ref[pack * TILE : (pack + 1) * TILE, at, b], 0, 1)
                    for b in range(blocks)
                ]
                values.append(
                    SCALE * jnp.concatenate(parts, axis=2).reshape(TILE * TILE, blocks * LANES)
                )
        result = permute(jnp.concatenate(values, axis=0), deal)
        at = 0
        for tile in range(low, high):
            for pack in range(packs):
                field[0, pack, (tile + 1) * TILE : (tile + 2) * TILE] = result[
                    at : at + TILE * TILE
                ].reshape(TILE, TILE, blocks * LANES)
                at += TILE * TILE

    upper = lax.broadcasted_iota(jnp.int32, (blocks, TILE, LANES), 1) < PATCH_ROWS

    def gather(index):
        base, count = chunks[index]
        for tile in range(base, base + count):
            for pack in range(packs):
                for b, part in enumerate(
                    split(field[0, pack, (tile + 1) * TILE : (tile + 2) * TILE])
                ):
                    first[pack * TILE : (pack + 1) * TILE, tile, b] = jnp.swapaxes(part, 0, 1)
        for tile in range(base, base + count):

            def body(g, carry, tile=tile):
                for slot in range(CAP):
                    even = lookup[slot, 2 * tile, g * per_dev]
                    odd = lookup[slot, 2 * tile + 1, g * per_dev]
                    send[g, tile, slot] = jnp.where(upper, first[even, tile], first[odd, tile])
                return carry

            lax.fori_loop(0, groups, body, 0)

    def scatter(index):
        base, count = chunks[index]
        recv = recvs[index]
        for tile in range(base, base + count):
            j = tile - base
            for pack in range(packs):
                children = []
                for k in range(pack * TILE, (pack + 1) * TILE):
                    at = me * per_dev + k
                    even = recv[lookup[2, 2 * tile, at], j, lookup[3, 2 * tile, at]]
                    odd = recv[lookup[2, 2 * tile + 1, at], j, lookup[3, 2 * tile + 1, at]]
                    children.append(jnp.where(upper, even, odd))
                for b in range(blocks):
                    mixed[
                        pack, (tile + 1) * TILE : (tile + 2) * TILE, :,
                        b * LANES : (b + 1) * LANES,
                    ] = jnp.swapaxes(jnp.stack([child[b] for child in children]), 0, 1)

    def blend(job):
        low, high = bounds(job, 0)
        for row, size in cut(low, high):
            at = row + TILE
            w = [weight[j, at : at + size] for j in range(3)]
            for pack in range(packs):
                near = [split(mixed[pack, at + j : at + j + size]) for j in range(-2, 3)]
                for b in range(blocks):
                    field[0, pack, at : at + size, :, b * LANES : (b + 1) * LANES] = (
                        w[0] * near[2][b]
                        + w[1] * (near[1][b] + near[3][b])
                        + w[2] * (near[0][b] + near[4][b])
                    )
        clear(field.at[0], low, high)

    def leave(low, high):
        return pltpu.make_async_copy(done.at[:, low:high], out.at[:, low:high], in_sem.at[6])

    def finish(low, high):
        values = [
            field[0, pack, (tile + 1) * TILE : (tile + 2) * TILE].reshape(
                TILE * TILE, blocks * LANES
            )
            for tile in range(low, high)
            for pack in range(packs)
        ]
        result = permute(jnp.concatenate(values, axis=0), undo)
        at = 0
        for tile in range(low, high):
            for pack in range(packs):
                parts = split(
                    result[at : at + TILE * TILE].reshape(TILE, TILE, blocks * LANES)
                )
                for b, part in enumerate(parts):
                    done[pack * TILE : (pack + 1) * TILE, tile, b] = jnp.swapaxes(part, 0, 1)
                at += TILE * TILE
            leave(tile, tile + 1).start()

    half = groups // 2
    if groups & (groups - 1):
        partners = [lax.rem(me + i, groups) for i in range(1, groups)]
    else:
        partners = [me ^ i for i in (*range(half, groups), *range(1, half))]

    def exchange_out(index):
        base, count = chunks[index]
        part = slice(base, base + count)
        for to in partners:
            pltpu.make_async_remote_copy(
                src_ref=send.at[to, part], dst_ref=recvs[index].at[me],
                send_sem=send_sem.at[0], recv_sem=recv_sem.at[index],
                device_id={"pgroup": to}, device_id_type=MESH,
            ).start()
        pltpu.make_async_copy(
            send.at[me, part], recvs[index].at[me], recv_sem.at[index]
        ).start()

    def exchange_in(index):
        base, count = chunks[index]
        part = slice(base, base + count)
        pltpu.make_async_copy(send.at[:, part], recvs[index], recv_sem.at[index]).wait()

    q = quarter
    fill_orders()
    inputs[4].wait()
    tables()
    to_lookup = pltpu.make_async_copy(table, lookup, in_sem.at[5])
    to_lookup.start()
    inputs[3].wait()
    fill_drive(2 * q - 2, 2 * q + 1)
    inputs[0].wait()
    load(2 * q - 2, 2 * q + 1)
    sweep((TILE * (2 * q - 1), TILE * 2 * q, False, False))
    to_lookup.wait()
    gather(0)
    pl.semaphore_wait(
        barrier, groups - 1 + has_low.astype(jnp.int32) + has_high.astype(jnp.int32)
    )
    inputs[5].wait()
    fill_kinds()

    @pl.when(has_high)
    def _():
        for upward, _ in edges:
            upward.start()

    @pl.when(has_low)
    def _():
        for _, downward in edges:
            downward.start()

    exchange_out(0)
    fill_edges()
    inputs[1].wait()
    fill_drive(0, 2 * q - 2)
    load(q - 1, 2 * q - 2)
    sweep((TILE * q, TILE * (2 * q - 1), False, True))
    gather(1)
    exchange_out(1)
    inputs[2].wait()
    fill_drive(2 * q + 1, tiles)

    @pl.when(has_low)
    def _():
        for upward, _ in edges:
            upward.wait_recv()

    @pl.when(has_high)
    def _():
        for _, downward in edges:
            downward.wait_recv()

    fill_drive(-1, 0)
    fill_drive(tiles, tiles + 1)
    load(-1, q - 1)
    sweep((0, TILE * q, False, True))
    gather(2)
    exchange_out(2)
    load(3 * q - 1, tiles + 1)
    sweep((TILE * 3 * q, extent, False, False))
    gather(3)
    exchange_out(3)
    load(2 * q + 1, 3 * q - 1)
    sweep((TILE * 2 * q, TILE * 3 * q, True, True))
    gather(4)
    exchange_out(4)
    gather(5)
    exchange_out(5)
    fill_weight(-TILE, extent + TILE)
    fill_returns()

    def second(job):
        blend(job)
        sweep(job)
        finish(job[0] // TILE, job[1] // TILE)

    for index in range(3):
        exchange_in(index)
        scatter(index)

    @pl.when(has_low)
    def _():
        middle[1].start()

    second((TILE, TILE * (2 * q - 1), False, False))
    exchange_in(3)
    scatter(3)

    @pl.when(has_high)
    def _():
        middle[0].start()

    @pl.when(has_high)
    def _():
        middle[1].wait_recv()

    second((TILE * (3 * q + 1), extent, False, False))
    exchange_in(4)
    scatter(4)
    second((TILE * (2 * q - 1), TILE * (3 * q - 2), True, False))

    @pl.when(has_low)
    def _():
        middle[0].wait_recv()

    second((0, TILE, False, True))
    exchange_in(5)
    scatter(5)
    second((TILE * (3 * q - 2), TILE * (3 * q + 1), True, True))

    leave(0, tiles).wait()

    @pl.when(has_high)
    def _():
        for upward, _ in edges:
            upward.wait_send()
        middle[0].wait_send()

    @pl.when(has_low)
    def _():
        for _, downward in edges:
            downward.wait_send()
        middle[1].wait_send()

    sent = slice(0, groups - 1)
    pltpu.make_async_remote_copy(
        src_ref=send.at[sent], dst_ref=send.at[sent],
        send_sem=send_sem.at[0], recv_sem=recv_sem.at[0],
        device_id={"pgroup": lax.rem(me + 1, groups)}, device_id_type=MESH,
    ).wait_send()


def settle(value):
    pieces = 8
    size = value.shape[0] // pieces

    def kernel(source, target, held, in_sem, out_sem):
        parts = [pl.ds(i * size, size) for i in range(pieces)]
        ins = [
            pltpu.make_async_copy(source.at[part], held.at[part], in_sem.at[i])
            for i, part in enumerate(parts)
        ]
        for copy in ins:
            copy.start()
        for copy, part in zip(ins, parts):
            copy.wait()
            pltpu.make_async_copy(held.at[part], target.at[part], out_sem).start()
        pltpu.make_async_copy(held, target, out_sem).wait()

    hbm = pl.BlockSpec(memory_space=pltpu.HBM)
    return pl.pallas_call(
        kernel,
        out_shape=jax.ShapeDtypeStruct(value.shape, value.dtype),
        in_specs=[hbm],
        out_specs=hbm,
        scratch_shapes=[
            pltpu.VMEM(value.shape, value.dtype),
            pltpu.SemaphoreType.DMA((pieces,)),
            pltpu.SemaphoreType.DMA,
        ],
        compiler_params=pltpu.CompilerParams(vmem_limit_bytes=VMEM),
        name="settle",
    )(value)


def on_device(state, forcing, parents, taper_index):
    per_dev, extent, width = state.shape
    bands, groups = lax.axis_size("band"), lax.axis_size("pgroup")
    blocks, tiles, packs = width // LANES, extent // TILE, per_dev // TILE
    state = state.reshape(per_dev, tiles, TILE, blocks, LANES).transpose(0, 1, 3, 2, 4)
    q = tiles // 4
    chunks = [
        (2 * q - 1, 1),
        (q, q - 1),
        (0, q),
        (3 * q, q),
        (2 * q, q - 1),
        (3 * q - 1, 1),
    ]
    rows = extent + 2 * TILE
    edge = (per_dev, 1, blocks, TILE, LANES)
    slot = (CAP, blocks, TILE, LANES)
    hbm = pl.BlockSpec(memory_space=pltpu.HBM)
    out = pl.pallas_call(
        functools.partial(kernel, bands, groups, chunks),
        out_shape=jax.ShapeDtypeStruct(state.shape, f32),
        in_specs=[hbm, hbm, hbm, hbm],
        out_specs=hbm,
        scratch_shapes=[
            pltpu.VMEM(state.shape, f32),
            pltpu.VMEM(state.shape, f32),
            pltpu.VMEM(forcing.shape, f32),
            pltpu.VMEM(parents.shape, jnp.int32),
            pltpu.SMEM(taper_index.shape, jnp.int32),
            pltpu.VMEM((extent, LANES), f32),
            pltpu.VMEM((4, *parents.shape), jnp.int32),
            pltpu.SMEM((4, *parents.shape), jnp.int32),
            pltpu.VMEM(state.shape, f32),
            pltpu.VMEM((2, packs, rows, TILE, width), f32),
            pltpu.VMEM((packs, rows, TILE, width), f32),
            pltpu.VMEM((rows, TILE, width), f32),
            pltpu.VMEM((3, rows, TILE, LANES), f32),
            pltpu.VMEM((2 * width, width), jnp.bfloat16),
            pltpu.VMEM((2 * width, width), jnp.bfloat16),
            pltpu.VMEM(edge, f32),
            pltpu.VMEM(edge, f32),
            pltpu.VMEM((TILE, width), f32),
            pltpu.VMEM((TILE, width), f32),
            pltpu.VMEM((TILE, LANES), f32),
            pltpu.VMEM((TILE, LANES), f32),
            pltpu.VMEM((groups, tiles, *slot), f32),
            pltpu.SemaphoreType.DMA((8,)),
            pltpu.SemaphoreType.DMA((8,)),
            pltpu.SemaphoreType.DMA((8,)),
            pltpu.SemaphoreType.DMA((1,)),
            pltpu.SemaphoreType.DMA((len(chunks),)),
            *[pltpu.VMEM((groups, count, *slot), f32) for _, count in chunks],
        ],
        compiler_params=pltpu.CompilerParams(
            collective_id=0, has_side_effects=True, vmem_limit_bytes=VMEM
        ),
        name="filter_step",
    )(state, forcing, parents, taper_index)
    out = settle(out)
    return out.transpose(0, 1, 3, 2, 4).reshape(per_dev, extent, width)


def solution(mesh):
    return jax.shard_map(
        on_device,
        mesh=mesh,
        in_specs=(P("pgroup", "band", None), P("band", None), P("band", None), P("band")),
        out_specs=P("pgroup", "band", None),
        check_vma=False,
    )
```

```python
import functools

import jax
import jax.numpy as jnp
from jax import lax
from jax.experimental import pallas as pl
from jax.experimental.pallas import tpu as pltpu
from jax.sharding import PartitionSpec as P

PATCH_ROWS = 4
STEPS = 6
CAP = 2
LANES = 128
TILE = 8
VMEM = 56 << 20
SCALE = 0.05
MESH = pl.DeviceIdType.MESH
f32 = jnp.float32


def cut(low, high, most=12):
    pieces = -(-(high - low) // most)
    marks = [low + (high - low) * i // pieces for i in range(pieces + 1)]
    return [(a, b - a) for a, b in zip(marks[:-1], marks[1:])]


def split(value):
    return [value[..., b * LANES : (b + 1) * LANES] for b in range(value.shape[-1] // LANES)]


def kernel(
    bands, groups, chunks, state, forcing, parents, taper_index, out,
    st, done, fo, par, taper, kinds, table, lookup, first, field, mixed, drive, weight, deal, undo,
    s_lo, s_hi, f_lo, f_hi, t_lo, t_hi, send,
    in_sem, halo_send, halo_recv, send_sem, recv_sem, *recvs,
):
    band, me = lax.axis_index("band"), lax.axis_index("pgroup")
    per_dev, tiles, blocks = state.shape[:3]
    extent, packs = tiles * TILE, per_dev // TILE
    patches = par.shape[0]
    quarter = tiles // 4
    has_low, has_high = band > 0, band < bands - 1
    up, down = lax.rem(band + 1, bands), lax.rem(band + bands - 1, bands)

    barrier = pltpu.get_barrier_semaphore()
    for step in range(1, groups):
        pl.semaphore_signal(
            barrier, inc=1, device_id={"pgroup": lax.rem(me + step, groups)}, device_id_type=MESH
        )

    @pl.when(has_low)
    def _():
        pl.semaphore_signal(barrier, inc=1, device_id={"band": down}, device_id_type=MESH)

    @pl.when(has_high)
    def _():
        pl.semaphore_signal(barrier, inc=1, device_id={"band": up}, device_id_type=MESH)

    def fetch(index, low, high):
        return pltpu.make_async_copy(
            state.at[:, low:high], st.at[:, low:high], in_sem.at[index]
        )

    inputs = [
        fetch(0, 2 * quarter - 2, 2 * quarter + 1),
        fetch(1, 0, 2 * quarter - 2),
        fetch(2, 2 * quarter + 1, tiles),
        pltpu.make_async_copy(forcing, fo, in_sem.at[3]),
        pltpu.make_async_copy(parents, par, in_sem.at[4]),
        pltpu.make_async_copy(taper_index, taper, in_sem.at[7]),
    ]
    for index in (4, 0, 3, 5, 1, 2):
        inputs[index].start()

    def halo(index, src, low, high, last, start):
        upward = pltpu.make_async_remote_copy(
            src_ref=src.at[last], dst_ref=low,
            send_sem=halo_send.at[2 * index], recv_sem=halo_recv.at[2 * index],
            device_id={"band": up}, device_id_type=MESH,
        )
        downward = pltpu.make_async_remote_copy(
            src_ref=src.at[start], dst_ref=high,
            send_sem=halo_send.at[2 * index + 1], recv_sem=halo_recv.at[2 * index + 1],
            device_id={"band": down}, device_id_type=MESH,
        )
        return upward, downward

    every = slice(None)
    bottom, top = slice(0, TILE), slice(extent - TILE, extent)
    edges = [
        halo(0, state, s_lo, s_hi, (every, slice(tiles - 1, tiles)), (every, slice(0, 1))),
        halo(1, forcing, f_lo, f_hi, (top,), (bottom,)),
        halo(2, kinds, t_lo, t_hi, (top,), (bottom,)),
    ]
    middle = halo(
        3, mixed, mixed.at[:, 0:TILE], mixed.at[:, extent + TILE : extent + 2 * TILE],
        (every, slice(extent, extent + TILE)), (every, slice(TILE, 2 * TILE)),
    )

    def fill_edges():
        @pl.when(jnp.logical_not(has_low))
        def _():
            for ref in (s_lo, f_lo, t_lo):
                ref[...] = jnp.zeros_like(ref)
            mixed[:, 0:TILE] = jnp.zeros((packs, TILE, TILE, blocks * LANES), f32)

        @pl.when(jnp.logical_not(has_high))
        def _():
            for ref in (s_hi, f_hi, t_hi):
                ref[...] = jnp.zeros_like(ref)
            mixed[:, extent + TILE : extent + 2 * TILE] = jnp.zeros(
                (packs, TILE, TILE, blocks * LANES), f32
            )

    lane = lax.broadcasted_iota(jnp.int32, (TILE, LANES), 1)
    run = LANES // blocks
    order = (lane % run) * blocks + lane // run

    def exchange(parts):
        parts = list(parts)
        span, count = LANES // 2, blocks // 2
        while count:
            near = (lane & span) == 0
            for j in range(blocks):
                if j & count:
                    continue
                a, b = parts[j], parts[j + count]
                parts[j] = jnp.where(near, a, pltpu.roll(b, span, 1))
                parts[j + count] = jnp.where(near, pltpu.roll(a, LANES - span, 1), b)
            span, count = span // 2, count // 2
        return parts

    def interleave(parts):
        return exchange([jnp.take_along_axis(part, order, axis=1) for part in parts])

    def fill_orders():
        width = blocks * LANES
        for half in range(width // LANES):
            rows = slice(half * LANES, (half + 1) * LANES)
            spot = lax.broadcasted_iota(jnp.int32, (LANES, width), 0) + half * LANES
            col = lax.broadcasted_iota(jnp.int32, (LANES, width), 1)
            there = jnp.where((spot % blocks) * LANES + spot // blocks == col, 1.0, 0.0)
            there = there.astype(jnp.bfloat16)
            deal[rows] = there
            deal[width + half * LANES : width + (half + 1) * LANES] = there

    def fill_returns():
        width = blocks * LANES
        for half in range(width // LANES):
            rows = slice(half * LANES, (half + 1) * LANES)
            spot = lax.broadcasted_iota(jnp.int32, (LANES, width), 0) + half * LANES
            col = lax.broadcasted_iota(jnp.int32, (LANES, width), 1)
            back = jnp.where((col % blocks) * LANES + col // blocks == spot, 1.0 / SCALE, 0.0)
            back = back.astype(jnp.bfloat16)
            undo[rows] = back
            undo[width + half * LANES : width + (half + 1) * LANES] = back

    def permute(value, matrix):
        high = value.astype(jnp.bfloat16)
        low = (value - high.astype(f32)).astype(jnp.bfloat16)
        return jnp.dot(
            jnp.concatenate([high, low], axis=1), matrix[...], preferred_element_type=f32
        )

    def tables():
        value = par[...]
        spot = lax.broadcasted_iota(jnp.int32, value.shape, 1) % per_dev
        owner, within = value // per_dev, value % per_dev
        mine = owner == me
        least = jnp.where(mine, within, per_dev - 1)
        most = jnp.where(mine, within, 0)
        reach = 1
        while reach < per_dev:
            least = jnp.minimum(least, pltpu.roll(least, value.shape[1] - reach, 1))
            most = jnp.maximum(most, pltpu.roll(most, value.shape[1] - reach, 1))
            reach *= 2
        rank = jnp.zeros_like(value)
        for reach in range(1, per_dev):
            ahead = pltpu.roll(value, value.shape[1] - reach, 1)
            behind = pltpu.roll(value, per_dev - reach, 1)
            other = jnp.where(spot + reach < per_dev, ahead, behind)
            below = (other // per_dev == owner) & (other < value)
            rank = jnp.where(below, 1, rank)
        table[0] = least
        table[1] = most
        table[2] = owner
        table[3] = rank

    def piece(low, mid, high, row):
        if row < 0:
            return low, row + TILE
        if row >= extent:
            return high, row - extent
        return mid, row

    sub = lax.broadcasted_iota(jnp.int32, (TILE, LANES), 0)

    def fill_kinds():
        for tile in range(tiles):
            value = jnp.zeros((TILE, LANES), f32)
            for r in range(TILE):
                value = jnp.where(sub == r, taper[tile * TILE + r].astype(f32), value)
            kinds[tile * TILE : (tile + 1) * TILE] = value

    def fill_drive(low, high):
        for tile in range(low, high):
            ref, at = piece(f_lo, fo, f_hi, tile * TILE)
            parts = interleave([SCALE * part for part in split(ref[at : at + TILE])])
            for b, part in enumerate(parts):
                for r in range(TILE):
                    drive[(tile + 1) * TILE + r, :, b * LANES : (b + 1) * LANES] = (
                        jnp.broadcast_to(part[r : r + 1], (TILE, LANES))
                    )

    def fill_weight(low, high):
        for row in range(low, high):
            ref, at = piece(t_lo, kinds, t_hi, row)
            kind = jnp.broadcast_to(ref[pl.ds(at, 1), :], (TILE, LANES)) + 1.0
            near, far = jnp.exp(-0.2 * kind), jnp.exp(-0.8 * kind)
            scale = 1.0 / (1.0 + 2.0 * near + 2.0 * far)
            weight[0, row + TILE] = scale
            weight[1, row + TILE] = near * scale
            weight[2, row + TILE] = far * scale

    def clear(ref, low, high):
        if low < 0:
            ref[:, TILE - 1] = jnp.where(has_low, ref[:, TILE - 1], 0.0)
        if high > extent:
            ref[:, TILE + extent] = jnp.where(has_high, ref[:, TILE + extent], 0.0)

    def bounds(job, step):
        low, high, left, right = job
        rest = STEPS - step
        return low + (rest if left else -rest), high - (rest if right else -rest)

    def advance(source, target, pack, at, size):
        c = split(source[pack, at : at + size])
        n = split(source[pack, at + 1 : at + size + 1])
        s = split(source[pack, at - 1 : at + size - 1])
        d = split(drive[at : at + size])
        wrap_e = pltpu.roll(c[0], LANES - 1, 2)
        wrap_w = pltpu.roll(c[-1], 1, 2)
        for b in range(blocks):
            e = c[b + 1] if b < blocks - 1 else wrap_e
            w = c[b - 1] if b else wrap_w
            target[pack, at : at + size, :, b * LANES : (b + 1) * LANES] = (
                c[b] * (0.4 - (e - w)) + 0.15 * (e + w)
            ) + ((0.05 * n[b] + 0.25 * s[b]) + d[b])

    def sweep(job):
        for step in range(1, STEPS + 1):
            low, high = bounds(job, step)
            source, target = field.at[(step - 1) % 2], field.at[step % 2]
            for row, size in cut(low, high):
                for pack in range(packs):
                    advance(source, target, pack, row + TILE, size)
            if step < STEPS:
                clear(target, low, high)

    def load(low, high):
        if low >= high:
            return
        values = []
        for tile in range(low, high):
            if tile < 0:
                ref, at = s_lo, 0
            elif tile >= tiles:
                ref, at = s_hi, 0
            else:
                ref, at = st, tile
            for pack in range(packs):
                parts = [
                    jnp.swapaxes(ref[pack * TILE : (pack + 1) * TILE, at, b], 0, 1)
                    for b in range(blocks)
                ]
                values.append(
                    SCALE * jnp.concatenate(parts, axis=2).reshape(TILE * TILE, blocks * LANES)
                )
        result = permute(jnp.concatenate(values, axis=0), deal)
        at = 0
        for tile in range(low, high):
            for pack in range(packs):
                field[0, pack, (tile + 1) * TILE : (tile + 2) * TILE] = result[
                    at : at + TILE * TILE
                ].reshape(TILE, TILE, blocks * LANES)
                at += TILE * TILE

    upper = lax.broadcasted_iota(jnp.int32, (blocks, TILE, LANES), 1) < PATCH_ROWS

    def gather(index):
        base, count = chunks[index]
        for tile in range(base, base + count):
            for pack in range(packs):
                for b, part in enumerate(
                    split(field[0, pack, (tile + 1) * TILE : (tile + 2) * TILE])
                ):
                    first[pack * TILE : (pack + 1) * TILE, tile, b] = jnp.swapaxes(part, 0, 1)
        for tile in range(base, base + count):

            def body(g, carry, tile=tile):
                for slot in range(CAP):
                    even = lookup[slot, 2 * tile, g * per_dev]
                    odd = lookup[slot, 2 * tile + 1, g * per_dev]
                    send[g, tile, slot] = jnp.where(upper, first[even, tile], first[odd, tile])
                return carry

            lax.fori_loop(0, groups, body, 0)

    def scatter(index):
        base, count = chunks[index]
        recv = recvs[index]
        for tile in range(base, base + count):
            j = tile - base
            for pack in range(packs):
                children = []
                for k in range(pack * TILE, (pack + 1) * TILE):
                    at = me * per_dev + k
                    even = recv[lookup[2, 2 * tile, at], j, lookup[3, 2 * tile, at]]
                    odd = recv[lookup[2, 2 * tile + 1, at], j, lookup[3, 2 * tile + 1, at]]
                    children.append(jnp.where(upper, even, odd))
                for b in range(blocks):
                    mixed[
                        pack, (tile + 1) * TILE : (tile + 2) * TILE, :,
                        b * LANES : (b + 1) * LANES,
                    ] = jnp.swapaxes(jnp.stack([child[b] for child in children]), 0, 1)

    def blend(job):
        low, high = bounds(job, 0)
        for row, size in cut(low, high):
            at = row + TILE
            w = [weight[j, at : at + size] for j in range(3)]
            for pack in range(packs):
                near = [split(mixed[pack, at + j : at + j + size]) for j in range(-2, 3)]
                for b in range(blocks):
                    field[0, pack, at : at + size, :, b * LANES : (b + 1) * LANES] = (
                        w[0] * near[2][b]
                        + w[1] * (near[1][b] + near[3][b])
                        + w[2] * (near[0][b] + near[4][b])
                    )
        clear(field.at[0], low, high)

    def leave(low, high):
        return pltpu.make_async_copy(done.at[:, low:high], out.at[:, low:high], in_sem.at[6])

    def finish(low, high):
        values = [
            field[0, pack, (tile + 1) * TILE : (tile + 2) * TILE].reshape(
                TILE * TILE, blocks * LANES
            )
            for tile in range(low, high)
            for pack in range(packs)
        ]
        result = permute(jnp.concatenate(values, axis=0), undo)
        at = 0
        for tile in range(low, high):
            for pack in range(packs):
                parts = split(
                    result[at : at + TILE * TILE].reshape(TILE, TILE, blocks * LANES)
                )
                for b, part in enumerate(parts):
                    done[pack * TILE : (pack + 1) * TILE, tile, b] = jnp.swapaxes(part, 0, 1)
                at += TILE * TILE
            leave(tile, tile + 1).start()

    half = groups // 2
    if groups & (groups - 1):
        partners = [lax.rem(me + i, groups) for i in range(1, groups)]
    else:
        partners = [me ^ i for i in (*range(half, groups), *range(1, half))]

    def exchange_out(index):
        base, count = chunks[index]
        part = slice(base, base + count)
        for to in partners:
            pltpu.make_async_remote_copy(
                src_ref=send.at[to, part], dst_ref=recvs[index].at[me],
                send_sem=send_sem.at[0], recv_sem=recv_sem.at[index],
                device_id={"pgroup": to}, device_id_type=MESH,
            ).start()
        pltpu.make_async_copy(
            send.at[me, part], recvs[index].at[me], recv_sem.at[index]
        ).start()

    def exchange_in(index):
        base, count = chunks[index]
        part = slice(base, base + count)
        pltpu.make_async_copy(send.at[:, part], recvs[index], recv_sem.at[index]).wait()

    q = quarter
    fill_orders()
    inputs[4].wait()
    tables()
    to_lookup = pltpu.make_async_copy(table, lookup, in_sem.at[5])
    to_lookup.start()
    inputs[3].wait()
    fill_drive(2 * q - 2, 2 * q + 1)
    inputs[0].wait()
    load(2 * q - 2, 2 * q + 1)
    sweep((TILE * (2 * q - 1), TILE * 2 * q, False, False))
    to_lookup.wait()
    gather(0)
    pl.semaphore_wait(
        barrier, groups - 1 + has_low.astype(jnp.int32) + has_high.astype(jnp.int32)
    )
    inputs[5].wait()
    fill_kinds()

    @pl.when(has_high)
    def _():
        for upward, _ in edges:
            upward.start()

    @pl.when(has_low)
    def _():
        for _, downward in edges:
            downward.start()

    exchange_out(0)
    fill_edges()
    inputs[1].wait()
    fill_drive(0, 2 * q - 2)
    load(q - 1, 2 * q - 2)
    sweep((TILE * q, TILE * (2 * q - 1), False, True))
    gather(1)
    exchange_out(1)
    inputs[2].wait()
    fill_drive(2 * q + 1, tiles)

    @pl.when(has_low)
    def _():
        for upward, _ in edges:
            upward.wait_recv()

    @pl.when(has_high)
    def _():
        for _, downward in edges:
            downward.wait_recv()

    fill_drive(-1, 0)
    fill_drive(tiles, tiles + 1)
    load(-1, q - 1)
    sweep((0, TILE * q, False, True))
    gather(2)
    exchange_out(2)
    load(3 * q - 1, tiles + 1)
    sweep((TILE * 3 * q, extent, False, False))
    gather(3)
    exchange_out(3)
    load(2 * q + 1, 3 * q - 1)
    sweep((TILE * 2 * q, TILE * 3 * q, True, True))
    gather(4)
    exchange_out(4)
    gather(5)
    exchange_out(5)
    fill_weight(-TILE, extent + TILE)
    fill_returns()

    def second(job):
        blend(job)
        sweep(job)
        finish(job[0] // TILE, job[1] // TILE)

    for index in range(3):
        exchange_in(index)
        scatter(index)

    @pl.when(has_low)
    def _():
        middle[1].start()

    second((TILE, TILE * (2 * q - 1), False, False))
    exchange_in(3)
    scatter(3)

    @pl.when(has_high)
    def _():
        middle[0].start()

    @pl.when(has_high)
    def _():
        middle[1].wait_recv()

    second((TILE * (3 * q + 1), extent, False, False))
    exchange_in(4)
    scatter(4)
    second((TILE * (2 * q - 1), TILE * (3 * q - 2), True, False))

    @pl.when(has_low)
    def _():
        middle[0].wait_recv()

    second((0, TILE, False, True))
    exchange_in(5)
    scatter(5)
    second((TILE * (3 * q - 2), TILE * (3 * q + 1), True, True))

    leave(0, tiles).wait()

    @pl.when(has_high)
    def _():
        for upward, _ in edges:
            upward.wait_send()
        middle[0].wait_send()

    @pl.when(has_low)
    def _():
        for _, downward in edges:
            downward.wait_send()
        middle[1].wait_send()

    sent = slice(0, groups - 1)
    pltpu.make_async_remote_copy(
        src_ref=send.at[sent], dst_ref=send.at[sent],
        send_sem=send_sem.at[0], recv_sem=recv_sem.at[0],
        device_id={"pgroup": lax.rem(me + 1, groups)}, device_id_type=MESH,
    ).wait_send()


def settle(value):
    pieces = 8
    size = value.shape[0] // pieces

    def kernel(source, target, held, in_sem, out_sem):
        parts = [pl.ds(i * size, size) for i in range(pieces)]
        ins = [
            pltpu.make_async_copy(source.at[part], held.at[part], in_sem.at[i])
            for i, part in enumerate(parts)
        ]
        for copy in ins:
            copy.start()
        for copy, part in zip(ins, parts):
            copy.wait()
            pltpu.make_async_copy(held.at[part], target.at[part], out_sem).start()
        pltpu.make_async_copy(held, target, out_sem).wait()

    hbm = pl.BlockSpec(memory_space=pltpu.HBM)
    return pl.pallas_call(
        kernel,
        out_shape=jax.ShapeDtypeStruct(value.shape, value.dtype),
        in_specs=[hbm],
        out_specs=hbm,
        scratch_shapes=[
            pltpu.VMEM(value.shape, value.dtype),
            pltpu.SemaphoreType.DMA((pieces,)),
            pltpu.SemaphoreType.DMA,
        ],
        compiler_params=pltpu.CompilerParams(vmem_limit_bytes=VMEM),
        name="settle",
    )(value)


def on_device(state, forcing, parents, taper_index):
    per_dev, extent, width = state.shape
    bands, groups = lax.axis_size("band"), lax.axis_size("pgroup")
    blocks, tiles, packs = width // LANES, extent // TILE, per_dev // TILE
    state = state.reshape(per_dev, tiles, TILE, blocks, LANES).transpose(0, 1, 3, 2, 4)
    q = tiles // 4
    chunks = [
        (2 * q - 1, 1),
        (q, q - 1),
        (0, q),
        (3 * q, q),
        (2 * q, q - 1),
        (3 * q - 1, 1),
    ]
    rows = extent + 2 * TILE
    edge = (per_dev, 1, blocks, TILE, LANES)
    slot = (CAP, blocks, TILE, LANES)
    hbm = pl.BlockSpec(memory_space=pltpu.HBM)
    out = pl.pallas_call(
        functools.partial(kernel, bands, groups, chunks),
        out_shape=jax.ShapeDtypeStruct(state.shape, f32),
        in_specs=[hbm, hbm, hbm, hbm],
        out_specs=hbm,
        scratch_shapes=[
            pltpu.VMEM(state.shape, f32),
            pltpu.VMEM(state.shape, f32),
            pltpu.VMEM(forcing.shape, f32),
            pltpu.VMEM(parents.shape, jnp.int32),
            pltpu.SMEM(taper_index.shape, jnp.int32),
            pltpu.VMEM((extent, LANES), f32),
            pltpu.VMEM((4, *parents.shape), jnp.int32),
            pltpu.SMEM((4, *parents.shape), jnp.int32),
            pltpu.VMEM(state.shape, f32),
            pltpu.VMEM((2, packs, rows, TILE, width), f32),
            pltpu.VMEM((packs, rows, TILE, width), f32),
            pltpu.VMEM((rows, TILE, width), f32),
            pltpu.VMEM((3, rows, TILE, LANES), f32),
            pltpu.VMEM((2 * width, width), jnp.bfloat16),
            pltpu.VMEM((2 * width, width), jnp.bfloat16),
            pltpu.VMEM(edge, f32),
            pltpu.VMEM(edge, f32),
            pltpu.VMEM((TILE, width), f32),
            pltpu.VMEM((TILE, width), f32),
            pltpu.VMEM((TILE, LANES), f32),
            pltpu.VMEM((TILE, LANES), f32),
            pltpu.VMEM((groups, tiles, *slot), f32),
            pltpu.SemaphoreType.DMA((8,)),
            pltpu.SemaphoreType.DMA((8,)),
            pltpu.SemaphoreType.DMA((8,)),
            pltpu.SemaphoreType.DMA((1,)),
            pltpu.SemaphoreType.DMA((len(chunks),)),
            *[pltpu.VMEM((groups, count, *slot), f32) for _, count in chunks],
        ],
        compiler_params=pltpu.CompilerParams(
            collective_id=0, has_side_effects=True, vmem_limit_bytes=VMEM
        ),
        name="filter_step",
    )(state, forcing, parents, taper_index)
    out = settle(out)
    return out.transpose(0, 1, 3, 2, 4).reshape(per_dev, extent, width)


def solution(mesh):
    return jax.shard_map(
        on_device,
        mesh=mesh,
        in_specs=(P("pgroup", "band", None), P("band", None), P("band", None), P("band")),
        out_specs=P("pgroup", "band", None),
        check_vma=False,
    )
```
